32 devices in a mesh: gx: 4 (over z), gy: 2 (over x), gz: 4 (over y, core).
Axes of the slice: x: 2, y: 2, z: 4, core: 2. Of those that a mesh axis runs over, the one named last changes fastest.
Arguments:
- data: float32 [16, 512, 256], P('gz', 'gx', 'gy'), may hold values from -6 to 6
- weight: float32 [16, 512, 256], P('gz', 'gx', 'gy'), may hold values from 0.2 to 2
- dual_start: float32 [3, 16, 512, 256], P(None, 'gz', 'gx', 'gy'), may hold values from -3 to 3
- dual_mid: float32 [3, 16, 512, 256], P(None, 'gz', 'gx', 'gy'), may hold values from -3 to 3
- cotangent: float32 [3, 16, 512, 256], P(None, 'gz', 'gx', 'gy'), may hold values from -6 to 6
Outputs:
- dual_grad: float32 [3, 16, 512, 256], P(None, 'gz', 'gx', 'gy')
- weight_grad: float32 [16, 512, 256], P('gz', 'gx', 'gy')
- data_grad: float32 [16, 512, 256], P('gz', 'gx', 'gy')
The draws below stay inside these ranges and needn't reach their ends.
All inputs are finite; a program needn't handle non-finite values.
Results may differ from the reference program's by a relative error of at most 0.00002.
Values sent between devices are 32-bit elements; how exact they have to be, the bound alone decides.
No kernel may reach another device: no remote copies, remote signals or barrier semaphores. Data moves between devices by JAX's collectives and lax.ppermute only.
A program may use at most 64 MiB of HBM per device.

```python
import math
import jax
import jax.numpy as jnp
from jax import lax

NP = 16
NR = 512
NC = 256


def block_scale(stream_key, extent, split, least, largest):
    def one(dim, shards_of):
        heights = jax.random.uniform(jax.random.fold_in(jax.random.fold_in(stream_key, 6), dim), (shards_of,), jnp.float32, least / len(split), largest / len(split))
        return jnp.repeat(jnp.exp(heights), extent[dim] // shards_of).reshape((-1,) + (1,) * (len(extent) - dim - 1))

    loudness = one(*split[0])
    for cut in split[1:]:
        loudness = loudness * one(*cut)
    return loudness


def bell_draw(key, extent, spread, most, pieces=(), held_as=jnp.bfloat16):
    loudness = block_scale(key, extent, pieces, -0.22, 0.18) if pieces else 1.0
    result = jax.random.normal(key, extent, jnp.float32) * spread * loudness
    return jnp.minimum(jnp.maximum(result, -most), most).astype(held_as)


def setup_inputs(seed: int = 0) -> dict:
    keys = jax.random.split(jax.random.key(seed), 6)
    data = bell_draw(keys[0], (NP, NR, NC), 1.0, 6.0, ((0, 4), (1, 4), (2, 2)), jnp.float32)
    weight = jnp.clip(jnp.exp(math.log(2.0) - 2.3025851 * jax.random.uniform(keys[1], (NP, NR, NC), jnp.float32) ** block_scale(keys[1], (NP, NR, NC), ((0, 4), (1, 4), (2, 2)), -0.2, 0.2)), 0.2, 2.0)
    dual_start = bell_draw(keys[2], (3, NP, NR, NC), 0.5, 3.0, ((1, 4), (2, 4), (3, 2)), jnp.float32)
    dual_mid = bell_draw(keys[3], (3, NP, NR, NC), 0.5, 3.0, ((1, 4), (2, 4), (3, 2)), jnp.float32)
    cotangent = bell_draw(keys[4], (3, NP, NR, NC), 1.0, 6.0, ((1, 4), (2, 4), (3, 2)), jnp.float32)
    return dict(data=data, weight=weight, dual_start=dual_start, dual_mid=dual_mid, cotangent=cotangent)


step_size = 0.08
inverse_lambda = 0.5
smoothing = 0.01

def forward_diff(field, axis):
    count = field.shape[axis]
    after = jnp.concatenate([lax.slice_in_dim(field, 1, count, axis=axis), jnp.zeros_like(lax.slice_in_dim(field, 0, 1, axis=axis))], axis)
    return after - field

def backward_diff(field, axis):
    count = field.shape[axis]
    before = jnp.concatenate([jnp.zeros_like(lax.slice_in_dim(field, 0, 1, axis=axis)), lax.slice_in_dim(field, 0, count - 1, axis=axis)], axis)
    return field - before

def divergence(dual):
    total = backward_diff(dual[0], 0)
    total = total + backward_diff(dual[1], 1)
    return total + backward_diff(dual[2], 2)

def gradient(field):
    return jnp.stack([forward_diff(field, 0), forward_diff(field, 1), forward_diff(field, 2)])

def adjoint_step(dual, weight, data, cot):
    values = divergence(dual) - data * inverse_lambda
    slopes = gradient(values)
    norm = jnp.sqrt(lax.optimization_barrier(jnp.sum(slopes * slopes, axis=0)) + smoothing)
    denom = 1.0 + step_size * norm / weight
    update = (dual + step_size * slopes) / denom
    inner = lax.optimization_barrier(jnp.sum(cot * update, axis=0))
    weight_part = inner * step_size * norm / (denom * weight * weight)
    norm_scale = -inner * step_size / (denom * weight)
    slope_cot = step_size * cot / denom + norm_scale / norm * slopes
    value_cot = -divergence(slope_cot)
    dual_cot = cot / denom - gradient(value_cot)
    return (dual_cot, weight_part, -value_cot * inverse_lambda)

def reference(data, weight, dual_start, dual_mid, cotangent):
    cot_mid, weight_mid, data_mid = adjoint_step(dual_mid, weight, data, cotangent)
    cot_start, weight_start, data_start = adjoint_step(dual_start, weight, data, cot_mid)
    return (cot_start, weight_start + weight_mid, data_start + data_mid)
```

```python
import functools

import jax
import jax.numpy as jnp
from jax import lax
from jax.experimental import pallas as pl
from jax.experimental.pallas import tpu as pltpu
from jax.sharding import PartitionSpec as P

STEP = 0.08
INVERSE = 0.5
SMOOTH = 0.01

AFTER = (3, 3, 3, 2, 2, 2, 2, 2, 2, 2, 3)
BEFORE = (2, 3, 2, 1, 2, 1, 2, 2, 2, 2, 2)
FIELDS = len(AFTER)
WEIGHT, DATA = 9, 10
PAD = 16
SUB = 8
LANES = 128
GROUP = 16


class Link:
    def __init__(self, axis, count):
        place = lax.axis_index(axis)
        self.even = lax.rem(place, 2) == 0
        self.odd = jnp.logical_not(self.even)
        self.before = place > 0
        self.after = place < count - 1


def phases(count):
    return 1 if count == 2 else 2


def swap(values, axis, count, spare, spare_count):
    out = [lax.all_gather(values[0], axis, axis_index_groups=[[i, i + 1] for i in range(0, count, 2)])]
    if count > 2:
        at = lambda i, j: i * spare_count + j
        groups = [[at(i, j), at(i + 1, j)] for i in range(1, count - 1, 2) for j in range(spare_count)]
        groups += [[at(i, j), at(i, j + 1)] for i in (0, count - 1) for j in range(0, spare_count, 2)]
        out.append(lax.all_gather(values[1], (axis, spare), axis_index_groups=groups))
    return out


def send(link, outs, up, down):
    @pl.when(link.even)
    def _():
        up(outs[0])
        if len(outs) > 1:
            down(outs[1])

    @pl.when(link.odd)
    def _():
        down(outs[0])
        if len(outs) > 1:
            up(outs[1])


def receive(link, ins, before, after):
    pl.when(link.odd)(lambda: before(ins[0].at[0]))
    pl.when(link.even)(lambda: after(ins[0].at[1]))
    if len(ins) > 1:
        pl.when(jnp.logical_and(link.even, link.before))(lambda: before(ins[1].at[0]))
        pl.when(jnp.logical_and(link.odd, link.after))(lambda: after(ins[1].at[1]))
    pl.when(jnp.logical_not(link.before))(lambda: before(None))
    pl.when(jnp.logical_not(link.after))(lambda: after(None))


def lane_ids():
    return lax.broadcasted_iota(jnp.int32, (SUB, LANES), 1)


def turn(x, by):
    return pltpu.roll(x, by % LANES if isinstance(by, int) else lax.rem(by + 4 * LANES, LANES), 1)


def col_before(x, strip, k, lane):
    return jnp.where(lane == 0, turn(strip, -(GROUP * (k + 1) + 11)), turn(x, 1))


def col_after(x, strip, k, lane):
    return jnp.where(lane == LANES - 1, turn(strip, LANES - 1 - (GROUP * (k + 1) + 4)), turn(x, -1))


def sources(dm, ds, ct, w, d):
    return [(r, a) for r in (dm, ds, ct) for a in range(3)] + [(w, None), (d, None)]


def src_rows(source, k, rows):
    ref, a = source
    return ref[k, rows, :] if a is None else ref[a, k, rows, :]


def offsets():
    out, total = [], 0
    for f in range(FIELDS):
        out.append(total)
        total += AFTER[f]
    return out, total


def rows_out(counts, dm, ds, ct, w, d, *outs):
    planes, rows = d.shape[0], d.shape[1]
    src = sources(dm, ds, ct, w, d)
    offs, per = offsets()
    link = Link("gx", counts["gx"])

    def up(out):
        for f in range(FIELDS):
            for k in range(planes):
                out[pl.ds(per * k + offs[f], BEFORE[f]), :] = src_rows(src[f], k, pl.ds(rows - BEFORE[f], BEFORE[f]))

    def down(out):
        for f in range(FIELDS):
            for k in range(planes):
                out[pl.ds(per * k + offs[f], AFTER[f]), :] = src_rows(src[f], k, pl.ds(0, AFTER[f]))

    send(link, outs, up, down)


def slot(f):
    return f // 8, 4 * (f % 4) + 64 * ((f // 4) % 2)


def build(counts, dm, ds, ct, w, d, *refs):
    planes, rows = d.shape[0], d.shape[1]
    nx, ny = phases(counts["gx"]), phases(counts["gy"])
    got, (em, es), outs = refs[:nx], refs[nx : nx + 2], refs[nx + 2 :]
    src = sources(dm, ds, ct, w, d)
    offs, per = offsets()
    lane = lane_ids()

    def halo(start, counted, deep):
        def fill(ref):
            for f in range(FIELDS):
                for k in range(planes):
                    if ref is None:
                        at, many = start(deep), deep
                        value = jnp.full((deep, LANES), 1.0 if f == WEIGHT else 0.0, jnp.float32)
                    else:
                        at, many = start(counted[f]), counted[f]
                        value = ref[pl.ds(per * k + offs[f], many), :]
                    em[f, k, pl.ds(at, many), :] = value

        return fill

    receive(
        Link("gx", counts["gx"]),
        got,
        halo(lambda n: PAD - n, BEFORE, 3),
        halo(lambda n: PAD + rows, AFTER, 3),
    )
    link = Link("gy", counts["gy"])
    part = lax.rem(lane, GROUP) // 4
    plane_of = lane // GROUP

    def tile(row, read):
        packed = [[None, None] for _ in range(ny)]
        for f in range(FIELDS):
            strip = jnp.full((SUB, LANES), 1.0 if f == WEIGHT else 0.0, jnp.float32)
            for k in range(planes):
                x = read(f, k)
                base = GROUP * (k + 1)
                here = plane_of == k + 1
                strip = jnp.where(jnp.logical_and(here, part == 0), turn(x, base + 4), strip)
                strip = jnp.where(jnp.logical_and(here, part == 3), turn(x, base + 12), strip)
            es[f, pl.ds(row, SUB), :] = strip
            which, shift = slot(f)
            mask = jnp.logical_and(part == (f % 4), lane // 64 == (f // 4) % 2)
            for p in range(ny):
                up = link.even if p == 0 else link.odd
                moved = turn(strip, shift - GROUP + jnp.where(up, 0, -12))
                old = packed[p][which]
                packed[p][which] = moved if old is None else jnp.where(mask, moved, old)
        for p in range(ny):
            for which in range(2):
                outs[p][which, pl.ds(row - SUB, SUB), :] = packed[p][which]

    @pl.loop(0, rows // SUB)
    def _(t):
        inside = pl.multiple_of(t * SUB, SUB)
        row = pl.multiple_of(t * SUB + PAD, SUB)

        def read(f, k):
            x = src_rows(src[f], k, pl.ds(inside, SUB))
            em[f, k, pl.ds(row, SUB), :] = x
            return x

        tile(row, read)

    @pl.loop(0, 2)
    def _(t):
        row = pl.multiple_of(PAD - SUB + t * (rows + SUB), SUB)
        tile(row, lambda f, k: em[f, k, pl.ds(row, SUB), :])


def fold(strip, group, out, base, tiles):
    lane = lane_ids()
    many = LANES // GROUP

    @pl.loop(0, tiles)
    def _(t):
        side = lax.rem(t, many)
        at = pl.ds(pl.multiple_of(base + SUB * (t // many), SUB), SUB)
        x = strip[pl.ds(pl.multiple_of(SUB * t + SUB, SUB), SUB), :]
        out[at, :] = jnp.where(lane // GROUP == side, turn(x, GROUP * (side - group)), out[at, :])


def unfold(ref, base, t, group):
    many = LANES // GROUP
    x = ref[pl.ds(pl.multiple_of(base + SUB * (t // many), SUB), SUB), :]
    return turn(x, GROUP * (group - lax.rem(t, many)))


def sizes(rows):
    tiles = (rows + 2 * PAD - 2 * SUB) // SUB
    folded = SUB * pl.cdiv(tiles * GROUP, LANES)
    return tiles, SUB * tiles, folded


def copy_rows(src, out, base, tiles):
    @pl.loop(0, tiles)
    def _(t):
        out[pl.ds(pl.multiple_of(base + SUB * t, SUB), SUB), :] = src[pl.ds(pl.multiple_of(SUB * t + SUB, SUB), SUB), :]


def plane_out(link, outs, up, down, planes, rows):
    tiles, flat, folded = sizes(rows)

    def put(items, group):
        def write(out):
            for i, (plane, strip) in enumerate(items):
                base = i * (flat + folded)
                copy_rows(plane, out, base, tiles)
                fold(strip, group, out, base + flat, tiles)

        return write

    send(link, outs, put(up, planes), put(down, 1))


def plane_in(link, ins, below, above):
    def put(dst):
        def fill(ref):
            @pl.loop(0, dst.shape[0] // SUB)
            def _(t):
                at = pl.ds(pl.multiple_of(t * SUB, SUB), SUB)
                dst[at, :] = jnp.zeros((SUB, LANES), jnp.float32) if ref is None else ref[at, :]

        return fill

    receive(link, ins, put(below), put(above))


def strips_and_values(counts, em, es, *refs):
    planes, rows = em.shape[1], em.shape[2] - 2 * PAD
    ny = phases(counts["gy"])
    got, (full, v, vs), outs = refs[:ny], refs[ny : ny + 3], refs[ny + 3 :]
    link = Link("gy", counts["gy"])
    row_link = Link("gx", counts["gx"])
    lane = lane_ids()
    part = lax.rem(lane, GROUP) // 4
    near = jnp.logical_or(part == 1, part == 2)
    real_after = jnp.logical_and(part == 1, link.after)
    real_before = jnp.logical_and(part == 2, link.before)
    lost = jnp.logical_and(part == 1, jnp.logical_not(link.after))
    inner = lane // GROUP >= 2
    tiles, flat, folded = sizes(rows)

    @pl.loop(0, tiles)
    def _(t):
        row = pl.multiple_of(SUB * t + SUB, SUB)
        at = pl.ds(pl.multiple_of(SUB * t, SUB), SUB)

        def sent(which, index):
            if ny == 1:
                return got[0][index, which, at, :]
            first = link.odd if index == 0 else link.even
            return jnp.where(first, got[0][index, which, at, :], got[1][index, which, at, :])

        blocks = [[sent(which, index) for which in range(2)] for index in range(2)]
        for f in range(FIELDS):
            which, shift = slot(f)
            x = jnp.where(near, 1.0 if f == WEIGHT else 0.0, es[f, pl.ds(row, SUB), :])
            x = jnp.where(real_after, turn(blocks[1][which], GROUP + 4 - shift), x)
            x = jnp.where(real_before, turn(blocks[0][which], GROUP + 8 - shift), x)
            full[f, pl.ds(row, SUB), :] = x

    @pl.loop(0, tiles)
    def _(t):
        row = pl.multiple_of(SUB * t + SUB, SUB)
        at, lower = pl.ds(row, SUB), pl.ds(row - 1, SUB)
        keep = jnp.logical_or(t < tiles - 1, row_link.after)
        for m in range(2):
            p0, p1, p2 = 3 * m, 3 * m + 1, 3 * m + 2
            s0, s2 = full[p0, at, :], full[p2, at, :]
            x = s0 - jnp.where(inner, turn(s0, GROUP), 0.0)
            x = x + (full[p1, at, :] - full[p1, lower, :])
            x = x + (s2 - turn(s2, 1))
            x = x - INVERSE * full[DATA, at, :]
            vs[m, at, :] = jnp.where(keep, jnp.where(lost, 0.0, x), 0.0)
            last = None
            for k in range(planes):
                x = now = em[p0, k, at, :]
                if k:
                    x = x - last
                last = now
                x = x + (em[p1, k, at, :] - em[p1, k, lower, :])
                y = em[p2, k, at, :]
                x = x + (y - col_before(y, s2, k, lane))
                x = x - INVERSE * em[DATA, k, at, :]
                v[m, k, at, :] = jnp.where(keep, x, 0.0)

    plane_out(
        Link("gz", counts["gz"]),
        outs,
        [(em.at[3 * m, planes - 1], full.at[3 * m]) for m in range(2)],
        [(v.at[m, 0], vs.at[m]) for m in range(2)],
        planes,
        rows,
    )


def settle(first, strip, last, last_strip, below, above, base, has_after, out_first, out_ghost, out_strip, planes, rows):
    tiles, flat, folded = sizes(rows)
    lane = lane_ids()
    group = lane // GROUP

    @pl.loop(0, tiles)
    def _(t):
        at = pl.ds(pl.multiple_of(SUB * t + SUB, SUB), SUB)
        sent = pl.ds(pl.multiple_of(base + SUB * t, SUB), SUB)
        out_first[at, :] = first[at, :] - below[sent, :]
        out_ghost[at, :] = jnp.where(has_after, above[sent, :] - last[at, :], 0.0)
        x = strip[at, :]
        x = jnp.where(group == 1, x - unfold(below, base + flat, t, 1), x)
        ghost = unfold(above, base + flat, t, planes + 1) - turn(last_strip[at, :], GROUP)
        ghost = jnp.where(has_after, ghost, 0.0)
        out_strip[at, :] = jnp.where(group == planes + 1, ghost, x)


def pointwise(g, c, p, w):
    q = g[0] * g[0] + g[1] * g[1] + g[2] * g[2] + SMOOTH
    rn = lax.rsqrt(q)
    tn = STEP * (q * rn)
    rw = 1.0 / w
    rden = 1.0 / (1.0 + tn * rw)
    inner = c[0] * p[0] + c[1] * p[1] + c[2] * p[2]
    inner = inner + STEP * (c[0] * g[0] + c[1] * g[1] + c[2] * g[2])
    s = inner * rden * (rden * rw)
    wpart = s * (tn * rw)
    scale = STEP * rden
    along = (-STEP) * s * rn
    return [scale * c[a] + along * g[a] for a in range(3)], rden, wpart


class Around:
    def __init__(self, plane, strip, planes, row, lane):
        self.plane, self.planes, self.lane = plane, planes, lane
        self.at, self.upper = pl.ds(row, SUB), pl.ds(row + 1, SUB)
        self.strip = strip
        self.s = strip[self.at, :]
        self.now = [plane(k)[self.at, :] for k in range(planes + 1)]

    def steps(self, k):
        x = self.now[k]
        return (
            self.now[k + 1] - x,
            self.plane(k)[self.upper, :] - x,
            col_after(x, self.s, k, self.lane) - x,
        )

    def strip_steps(self):
        x = self.s
        return turn(x, -GROUP) - x, self.strip[self.upper, :] - x, turn(x, -1) - x


class Back:
    def __init__(self, rows_ref, strip_ref, row, lane):
        self.rows_ref, self.strip_ref, self.lane = rows_ref, strip_ref, lane
        self.at, self.lower = pl.ds(row, SUB), pl.ds(row - 1, SUB)
        self.last = None

    def strip(self, cg):
        self.s = cg[2]
        self.strip_ref[self.at, :] = cg[1]
        x = cg[0] - jnp.where(self.lane // GROUP >= 2, turn(cg[0], GROUP), 0.0)
        x = x + (cg[1] - self.strip_ref[self.lower, :])
        return x + (cg[2] - turn(cg[2], 1))

    def plane(self, k, cg):
        self.rows_ref[k, self.at, :] = cg[1]
        x = cg[0] if self.last is None else cg[0] - self.last
        self.last = cg[0]
        x = x + (cg[1] - self.rows_ref[k, self.lower, :])
        return x + (cg[2] - col_before(cg[2], self.s, k, self.lane))


def chooser(mid, first, ghost, planes):
    return lambda k: first if k == 0 else ghost if k == planes else mid.at[k]


def first_step(counts, em, full, v, vs, *refs):
    planes, rows = em.shape[1], em.shape[2] - 2 * PAD
    nz = phases(counts["gz"])
    got, refs = refs[:nz], refs[nz:]
    (r, rs, rd, rds, wp, top, tops), outs, scratch = refs[:7], refs[7 : 7 + nz], refs[7 + nz :]
    below, above, first, ghost, strip, rows_ref, strip_ref = scratch
    link, row_link, col_link = (Link(a, counts[a]) for a in ("gz", "gx", "gy"))
    lane = lane_ids()
    lost = jnp.logical_and(lax.rem(lane, GROUP) // 4 == 1, jnp.logical_not(col_link.after))
    tiles, flat, folded = sizes(rows)
    plane_in(link, got, below, above)
    settle(v.at[0, 0], vs.at[0], em.at[0, planes - 1], full.at[0], below, above, 0, link.after, first, ghost, strip, planes, rows)

    @pl.loop(0, tiles)
    def _(t):
        row = pl.multiple_of(SUB * t + SUB, SUB)
        at = pl.ds(row, SUB)
        keep = jnp.logical_or(t < tiles - 1, row_link.after)
        field = Around(chooser(v.at[0], first, ghost, planes), strip, planes, row, lane)
        back = Back(rows_ref, strip_ref, row, lane)
        cg, rden, _ = pointwise(
            field.strip_steps(), [full[6 + a, at, :] for a in range(3)], [full[a, at, :] for a in range(3)], full[WEIGHT, at, :]
        )
        rds[at, :] = rden
        tops[at, :] = cg[0]
        rs[at, :] = jnp.where(keep, jnp.where(lost, 0.0, back.strip(cg)), 0.0)
        for k in range(planes):
            cg, rden, wpart = pointwise(
                field.steps(k), [em[6 + a, k, at, :] for a in range(3)], [em[a, k, at, :] for a in range(3)], em[WEIGHT, k, at, :]
            )
            rd[k, at, :] = rden
            wp[k, at, :] = wpart
            r[k, at, :] = jnp.where(keep, back.plane(k, cg), 0.0)
            if k == planes - 1:
                top[at, :] = cg[0]

    plane_out(link, outs, [(top, tops)], [(r.at[0], rs)], planes, rows)


def second_step(counts, em, full, v, vs, *refs):
    planes, rows = em.shape[1], em.shape[2] - 2 * PAD
    nz = phases(counts["gz"])
    got_v, refs = refs[:nz], refs[nz:]
    (r1, r1s, rd, rds, wp, top1, top1s), refs = refs[:7], refs[7:]
    got_r, refs = refs[:nz], refs[nz:]
    (x, r2, r2s, top, tops, wg, dg), outs, scratch = refs[:7], refs[7 : 7 + nz], refs[7 + nz :]
    below, above, below_r, above_r, first, ghost, strip, first_r, ghost_r, strip_r, rows_ref, strip_ref = scratch
    link, row_link, col_link = (Link(a, counts[a]) for a in ("gz", "gx", "gy"))
    lane = lane_ids()
    part = lax.rem(lane, GROUP) // 4
    lost = jnp.logical_and(part == 1, jnp.logical_not(col_link.after))
    outside = jnp.logical_and(part == 2, jnp.logical_not(col_link.before))
    tiles, flat, folded = sizes(rows)
    plane_in(link, got_v, below, above)
    settle(
        v.at[1, 0], vs.at[1], em.at[3, planes - 1], full.at[3], below, above, flat + folded, link.after, first, ghost, strip, planes, rows
    )
    plane_in(link, got_r, below_r, above_r)
    settle(r1.at[0], r1s, top1, top1s, below_r, above_r, 0, link.after, first_r, ghost_r, strip_r, planes, rows)

    @pl.loop(0, tiles)
    def _(t):
        row = pl.multiple_of(SUB * t + SUB, SUB)
        at = pl.ds(row, SUB)
        keep = jnp.logical_or(t < tiles - 1, row_link.after)
        inside = jnp.logical_or(t > 0, row_link.before)
        field = Around(chooser(v.at[1], first, ghost, planes), strip, planes, row, lane)
        spread = Around(chooser(r1, first_r, ghost_r, planes), strip_r, planes, row, lane)
        back = Back(rows_ref, strip_ref, row, lane)

        rden = rds[at, :]
        down = spread.strip_steps()
        c = [jnp.where(inside, jnp.where(outside, 0.0, full[6 + a, at, :] * rden + down[a]), 0.0) for a in range(3)]
        cg, _, _ = pointwise(field.strip_steps(), c, [full[3 + a, at, :] for a in range(3)], full[WEIGHT, at, :])
        tops[at, :] = cg[0]
        r2s[at, :] = jnp.where(keep, jnp.where(lost, 0.0, back.strip(cg)), 0.0)
        for k in range(planes):
            rden = rd[k, at, :]
            down = spread.steps(k)
            c = [jnp.where(inside, em[6 + a, k, at, :] * rden + down[a], 0.0) for a in range(3)]
            cg, rden, wpart = pointwise(field.steps(k), c, [em[3 + a, k, at, :] for a in range(3)], em[WEIGHT, k, at, :])
            for a in range(3):
                x[a, k, at, :] = c[a] * rden
            wg[k, at, :] = wp[k, at, :] + wpart
            dg[k, at, :] = spread.now[k]
            r2[k, at, :] = jnp.where(keep, back.plane(k, cg), 0.0)
            if k == planes - 1:
                top[at, :] = cg[0]

    plane_out(link, outs, [(top, tops)], [(r2.at[0], r2s)], planes, rows)


def finish(counts, x, r2, r2s, top, tops, wg, dg, *refs):
    planes, rows = r2.shape[0], r2.shape[1] - 2 * PAD
    nz = phases(counts["gz"])
    got, (grad, weight_grad, data_grad), scratch = refs[:nz], refs[nz : nz + 3], refs[nz + 3 :]
    below, above, first, ghost, strip = scratch
    link = Link("gz", counts["gz"])
    lane = lane_ids()
    plane_in(link, got, below, above)
    settle(r2.at[0], r2s, top, tops, below, above, 0, link.after, first, ghost, strip, planes, rows)

    @pl.loop(0, rows // SUB)
    def _(t):
        row = pl.multiple_of(SUB * t + PAD, SUB)
        at, to = pl.ds(row, SUB), pl.ds(pl.multiple_of(SUB * t, SUB), SUB)
        spread = Around(chooser(r2, first, ghost, planes), strip, planes, row, lane)
        for k in range(planes):
            down = spread.steps(k)
            for a in range(3):
                grad[a, k, to, :] = x[a, k, at, :] + down[a]
            weight_grad[k, to, :] = wg[k, at, :]
            data_grad[k, to, :] = INVERSE * (dg[k, at, :] + spread.now[k])


def call(body, counts, operands, outs, scratch=()):
    held = pl.BlockSpec(memory_space=pltpu.VMEM)
    return pl.pallas_call(
        functools.partial(body, counts),
        out_shape=outs,
        in_specs=[held] * len(operands),
        out_specs=[held] * len(outs),
        scratch_shapes=list(scratch),
        compiler_params=pltpu.CompilerParams(vmem_limit_bytes=16 * 1024 * 1024),
        name=body.__name__,
    )(*operands)


def vmem(*shape):
    return pltpu.VMEM(shape, jnp.float32)


def shards(counts, data, weight, dual_start, dual_mid, cotangent):
    planes, rows, cols = data.shape
    held = rows + 2 * PAD
    tiles, flat, folded = sizes(rows)
    nx, ny, nz = (phases(counts[a]) for a in ("gx", "gy", "gz"))
    raw = (dual_mid, dual_start, cotangent, weight, data)
    block, strip, line = vmem(planes, held, cols), vmem(held, LANES), vmem(held, cols)

    sent = call(rows_out, counts, raw, [vmem(planes * offsets()[1], cols)] * nx)
    got = swap(sent, "gx", counts["gx"], "gy", counts["gy"])
    em, es, *sent = call(
        build, counts, (*raw, *got), [vmem(FIELDS, planes, held, cols), vmem(FIELDS, held, LANES)] + [vmem(2, flat, LANES)] * ny
    )
    got = swap(sent, "gy", counts["gy"], "gx", counts["gx"])
    one = flat + folded
    full, v, vs, *sent = call(
        strips_and_values,
        counts,
        (em, es, *got),
        [vmem(FIELDS, held, LANES), vmem(2, planes, held, cols), vmem(2, held, LANES)] + [vmem(2 * one, LANES)] * nz,
    )
    got_v = swap(sent, "gz", counts["gz"], "gy", counts["gy"])
    state = [block, strip, block, strip, block, line, strip]
    work = [line, line, strip]
    *first, = call(
        first_step,
        counts,
        (em, full, v, vs, *got_v),
        state + [vmem(one, LANES)] * nz,
        [vmem(2 * one, LANES)] * 2 + work + [block, strip],
    )
    got_r = swap(first[7:], "gz", counts["gz"], "gy", counts["gy"])
    *second, = call(
        second_step,
        counts,
        (em, full, v, vs, *got_v, *first[:7], *got_r),
        [vmem(3, planes, held, cols), block, strip, line, strip, block, block] + [vmem(one, LANES)] * nz,
        [vmem(2 * one, LANES)] * 2 + [vmem(one, LANES)] * 2 + work + work + [block, strip],
    )
    got = swap(second[7:], "gz", counts["gz"], "gy", counts["gy"])
    out = jax.ShapeDtypeStruct
    return tuple(call(
        finish,
        counts,
        (*second[:7], *got),
        [out(dual_mid.shape, jnp.float32), out(data.shape, jnp.float32), out(data.shape, jnp.float32)],
        [vmem(one, LANES)] * 2 + work,
    ))


def solution(mesh):
    field, dual = P("gz", "gx", "gy"), P(None, "gz", "gx", "gy")
    return jax.shard_map(
        functools.partial(shards, dict(mesh.shape)),
        mesh=mesh,
        in_specs=(field, field, dual, dual, dual),
        out_specs=(dual, field, field),
        check_vma=False,
    )
```

```python
import functools

import jax
import jax.numpy as jnp
from jax import lax
from jax.experimental import pallas as pl
from jax.experimental.pallas import tpu as pltpu
from jax.sharding import PartitionSpec as P

STEP = 0.08
INVERSE = 0.5
SMOOTH = 0.01

AFTER = (3, 3, 3, 2, 2, 2, 2, 2, 2, 2, 3)
BEFORE = (2, 3, 2, 1, 2, 1, 2, 2, 2, 2, 2)
FIELDS = len(AFTER)
WEIGHT, DATA = 9, 10
PAD = 16
SUB = 8
UNROLL = 3
LANES = 128
GROUP = 16


class Link:
    def __init__(self, axis, count):
        place = lax.axis_index(axis)
        self.even = lax.rem(place, 2) == 0
        self.odd = jnp.logical_not(self.even)
        self.before = place > 0
        self.after = place < count - 1


def phases(count):
    return 1 if count == 2 else 2


def swap(values, axis, count, spare, spare_count):
    out = [lax.all_gather(values[0], axis, axis_index_groups=[[i, i + 1] for i in range(0, count, 2)])]
    if count > 2:
        at = lambda i, j: i * spare_count + j
        groups = [[at(i, j), at(i + 1, j)] for i in range(1, count - 1, 2) for j in range(spare_count)]
        groups += [[at(i, j), at(i, j + 1)] for i in (0, count - 1) for j in range(0, spare_count, 2)]
        out.append(lax.all_gather(values[1], (axis, spare), axis_index_groups=groups))
    return out


def send(link, outs, up, down):
    @pl.when(link.even)
    def _():
        up(outs[0])
        if len(outs) > 1:
            down(outs[1])

    @pl.when(link.odd)
    def _():
        down(outs[0])
        if len(outs) > 1:
            up(outs[1])


def receive(link, ins, before, after):
    pl.when(link.odd)(lambda: before(ins[0].at[0]))
    pl.when(link.even)(lambda: after(ins[0].at[1]))
    if len(ins) > 1:
        pl.when(jnp.logical_and(link.even, link.before))(lambda: before(ins[1].at[0]))
        pl.when(jnp.logical_and(link.odd, link.after))(lambda: after(ins[1].at[1]))
    pl.when(jnp.logical_not(link.before))(lambda: before(None))
    pl.when(jnp.logical_not(link.after))(lambda: after(None))


class Later:
    def __init__(self):
        self.items = []

    def put(self, ref, index, value):
        self.items.append((ref, index, value))

    def flush(self):
        for ref, index, value in self.items:
            ref[index] = value


ALL = slice(None)


def batches(count, size):
    return [range(i, min(i + size, count)) for i in range(0, count, size)]


def lane_ids():
    return lax.broadcasted_iota(jnp.int32, (SUB, LANES), 1)


def turn(x, by):
    return pltpu.roll(x, by % LANES if isinstance(by, int) else lax.rem(by + 4 * LANES, LANES), 1)


def col_before(x, strip, k, lane):
    return jnp.where(lane == 0, turn(strip, -(GROUP * (k + 1) + 11)), turn(x, 1))


def col_after(x, strip, k, lane):
    return jnp.where(lane == LANES - 1, turn(strip, LANES - 1 - (GROUP * (k + 1) + 4)), turn(x, -1))


def sources(dm, ds, ct, w, d):
    return [(r, a) for r in (dm, ds, ct) for a in range(3)] + [(w, None), (d, None)]


def src_rows(source, k, rows):
    ref, a = source
    return ref[k, rows, :] if a is None else ref[a, k, rows, :]


def offsets():
    out, total = [], 0
    for f in range(FIELDS):
        out.append(total)
        total += AFTER[f]
    return out, total


def rows_out(counts, *refs):
    nx = phases(counts["gx"])
    raw, outs, (*edges, sems) = refs[:5], refs[5 : 5 + nx], refs[5 + nx :]
    planes, rows = raw[4].shape[0], raw[4].shape[1]
    copies = []
    for i, ref in enumerate(raw):
        for end, at in enumerate((0, rows - SUB)):
            rows_at = pl.ds(at, SUB)
            view = ref.at[:, :, rows_at, :] if len(ref.shape) == 4 else ref.at[:, rows_at, :]
            copies.append(pltpu.make_async_copy(view, edges[2 * i + end], sems.at[2 * i + end]))
    for copy in copies:
        copy.start()
    for copy in copies:
        copy.wait()
    head, tail = sources(*edges[0::2]), sources(*edges[1::2])
    offs, per = offsets()

    def up(out):
        for f in range(FIELDS):
            for k in range(planes):
                out[pl.ds(per * k + offs[f], BEFORE[f]), :] = src_rows(tail[f], k, pl.ds(SUB - BEFORE[f], BEFORE[f]))

    def down(out):
        for f in range(FIELDS):
            for k in range(planes):
                out[pl.ds(per * k + offs[f], AFTER[f]), :] = src_rows(head[f], k, pl.ds(0, AFTER[f]))

    send(Link("gx", counts["gx"]), outs, up, down)


def slot(f):
    return f // 8, 4 * (f % 4) + 64 * ((f // 4) % 2)


def build(counts, dm, ds, ct, w, d, *refs):
    planes, rows = d.shape[0], d.shape[1]
    nx, ny = phases(counts["gx"]), phases(counts["gy"])
    got, (em, es), outs = refs[:nx], refs[nx : nx + 2], refs[nx + 2 :]
    src = sources(dm, ds, ct, w, d)
    offs, per = offsets()
    lane = lane_ids()

    def halo(start, counted, deep):
        def fill(ref):
            for f in range(FIELDS):
                for k in range(planes):
                    if ref is None:
                        at, many = start(deep), deep
                        value = jnp.full((deep, LANES), 1.0 if f == WEIGHT else 0.0, jnp.float32)
                    else:
                        at, many = start(counted[f]), counted[f]
                        value = ref[pl.ds(per * k + offs[f], many), :]
                    em[f, k, pl.ds(at, many), :] = value

        return fill

    receive(
        Link("gx", counts["gx"]),
        got,
        halo(lambda n: PAD - n, BEFORE, 3),
        halo(lambda n: PAD + rows, AFTER, 3),
    )
    link = Link("gy", counts["gy"])
    part = lax.rem(lane, GROUP) // 4
    plane_of = lane // GROUP

    def tile(row, read):
        packed = [[None, None] for _ in range(ny)]
        later = Later()
        for f in range(FIELDS):
            strip = jnp.full((SUB, LANES), 1.0 if f == WEIGHT else 0.0, jnp.float32)
            for k in range(planes):
                x = read(f, k)
                base = GROUP * (k + 1)
                here = plane_of == k + 1
                strip = jnp.where(jnp.logical_and(here, part == 0), turn(x, base + 4), strip)
                strip = jnp.where(jnp.logical_and(here, part == 3), turn(x, base + 12), strip)
            later.put(es, (f, pl.ds(row, SUB), ALL), strip)
            which, shift = slot(f)
            mask = jnp.logical_and(part == (f % 4), lane // 64 == (f // 4) % 2)
            for p in range(ny):
                up = link.even if p == 0 else link.odd
                moved = turn(strip, shift - GROUP + jnp.where(up, 0, -12))
                old = packed[p][which]
                packed[p][which] = moved if old is None else jnp.where(mask, moved, old)
        for p in range(ny):
            for which in range(2):
                later.put(outs[p], (which, pl.ds(row - SUB, SUB), ALL), packed[p][which])
        later.flush()

    @pl.loop(0, rows // SUB)
    def _(t):
        inside = pl.multiple_of(t * SUB, SUB)
        row = pl.multiple_of(t * SUB + PAD, SUB)

        def read(f, k):
            x = src_rows(src[f], k, pl.ds(inside, SUB))
            em[f, k, pl.ds(row, SUB), :] = x
            return x

        tile(row, read)

    @pl.loop(0, 2)
    def _(t):
        row = pl.multiple_of(PAD - SUB + t * (rows + SUB), SUB)
        tile(row, lambda f, k: em[f, k, pl.ds(row, SUB), :])


def fold(strip, group, out, base, tiles):
    group_of = lane_ids() // GROUP
    many = LANES // GROUP
    later = Later()
    for i, some in enumerate(batches(tiles, many)):
        x = None
        for t in some:
            y = turn(strip[pl.ds(SUB * t + SUB, SUB), :], GROUP * (t % many - group))
            x = y if x is None else jnp.where(group_of == t % many, y, x)
        later.put(out, (pl.ds(base + SUB * i, SUB), ALL), x)
    later.flush()


def unfold(read, base, t, group):
    many = LANES // GROUP
    return turn(read(base + SUB * (t // many)), GROUP * (group - t % many))


def sizes(rows):
    tiles = (rows + 2 * PAD - 2 * SUB) // SUB
    folded = SUB * pl.cdiv(tiles * GROUP, LANES)
    return tiles, SUB * tiles, folded


def copy_rows(src, out, base, tiles):
    for some in batches(tiles, 9):
        later = Later()
        for t in some:
            later.put(out, (pl.ds(base + SUB * t, SUB), ALL), src[pl.ds(SUB * t + SUB, SUB), :])
        later.flush()


def plane_out(link, outs, up, down, planes, rows):
    tiles, flat, folded = sizes(rows)

    def put(items, group):
        def write(out):
            for i, (plane, strip) in enumerate(items):
                base = i * (flat + folded)
                copy_rows(plane, out, base, tiles)
                fold(strip, group, out, base + flat, tiles)

        return write

    send(link, outs, put(up, planes), put(down, 1))


def plane_in(link, ins):
    def at(index, first, known):
        def read(row):
            x = ins[0][index, pl.ds(row, SUB), :]
            if len(ins) > 1:
                x = jnp.where(first, x, ins[1][index, pl.ds(row, SUB), :])
            return jnp.where(known, x, 0.0)

        return read

    return at(0, link.odd, link.before), at(1, link.even, link.after)


def strips_and_values(counts, em, es, *refs):
    planes, rows = em.shape[1], em.shape[2] - 2 * PAD
    ny = phases(counts["gy"])
    got, (full, v, vs), outs = refs[:ny], refs[ny : ny + 3], refs[ny + 3 :]
    link = Link("gy", counts["gy"])
    row_link = Link("gx", counts["gx"])
    lane = lane_ids()
    part = lax.rem(lane, GROUP) // 4
    near = jnp.logical_or(part == 1, part == 2)
    real_after = jnp.logical_and(part == 1, link.after)
    real_before = jnp.logical_and(part == 2, link.before)
    lost = jnp.logical_and(part == 1, jnp.logical_not(link.after))
    inner = lane // GROUP >= 2
    tiles, flat, folded = sizes(rows)

    def strips(t, later):
        row = pl.multiple_of(SUB * t + SUB, SUB)
        at = pl.ds(pl.multiple_of(SUB * t, SUB), SUB)

        def sent(which, index):
            if ny == 1:
                return got[0][index, which, at, :]
            first = link.odd if index == 0 else link.even
            return jnp.where(first, got[0][index, which, at, :], got[1][index, which, at, :])

        blocks = [[sent(which, index) for which in range(2)] for index in range(2)]
        for f in range(FIELDS):
            which, shift = slot(f)
            x = jnp.where(near, 1.0 if f == WEIGHT else 0.0, es[f, pl.ds(row, SUB), :])
            x = jnp.where(real_after, turn(blocks[1][which], GROUP + 4 - shift), x)
            x = jnp.where(real_before, turn(blocks[0][which], GROUP + 8 - shift), x)
            later.put(full, (f, pl.ds(row, SUB), ALL), x)

    def values(t, later):
        row = pl.multiple_of(SUB * t + SUB, SUB)
        at, lower = pl.ds(row, SUB), pl.ds(row - 1, SUB)
        keep = jnp.logical_or(t < tiles - 1, row_link.after)
        for m in range(2):
            p0, p1, p2 = 3 * m, 3 * m + 1, 3 * m + 2
            s0, s2 = full[p0, at, :], full[p2, at, :]
            x = s0 - jnp.where(inner, turn(s0, GROUP), 0.0)
            x = x + (full[p1, at, :] - full[p1, lower, :])
            x = x + (s2 - turn(s2, 1))
            x = x - INVERSE * full[DATA, at, :]
            later.put(vs, (m, at, ALL), jnp.where(keep, jnp.where(lost, 0.0, x), 0.0))
            last = None
            for k in range(planes):
                x = now = em[p0, k, at, :]
                if k:
                    x = x - last
                last = now
                x = x + (em[p1, k, at, :] - em[p1, k, lower, :])
                y = em[p2, k, at, :]
                x = x + (y - col_before(y, s2, k, lane))
                x = x - INVERSE * em[DATA, k, at, :]
                later.put(v, (m, k, at, ALL), jnp.where(keep, x, 0.0))

    for body in (strips, values):

        @pl.loop(0, tiles // UNROLL)
        def _(t):
            later = Later()
            for u in range(UNROLL):
                body(t * UNROLL + u, later)
            later.flush()

    plane_out(
        Link("gz", counts["gz"]),
        outs,
        [(em.at[3 * m, planes - 1], full.at[3 * m]) for m in range(2)],
        [(v.at[m, 0], vs.at[m]) for m in range(2)],
        planes,
        rows,
    )


def settle(first, strip, last, last_strip, below, above, base, has_after, out_first, out_ghost, out_strip, planes, rows):
    tiles, flat, folded = sizes(rows)
    group = lane_ids() // GROUP
    for some in batches(tiles, 6):
        later = Later()
        for t in some:
            at = (pl.ds(SUB * t + SUB, SUB), ALL)
            sent = base + SUB * t
            later.put(out_first, at, first[at] - below(sent))
            later.put(out_ghost, at, jnp.where(has_after, above(sent) - last[at], 0.0))
            x = strip[at]
            x = jnp.where(group == 1, x - unfold(below, base + flat, t, 1), x)
            ghost = unfold(above, base + flat, t, planes + 1) - turn(last_strip[at], GROUP)
            ghost = jnp.where(has_after, ghost, 0.0)
            later.put(out_strip, at, jnp.where(group == planes + 1, ghost, x))
        later.flush()


def pointwise(g, c, p, w):
    q = g[0] * g[0] + g[1] * g[1] + g[2] * g[2] + SMOOTH
    rn = lax.rsqrt(q)
    tn = STEP * (q * rn)
    rw = 1.0 / w
    rden = 1.0 / (1.0 + tn * rw)
    inner = c[0] * p[0] + c[1] * p[1] + c[2] * p[2]
    inner = inner + STEP * (c[0] * g[0] + c[1] * g[1] + c[2] * g[2])
    s = inner * rden * (rden * rw)
    wpart = s * (tn * rw)
    scale = STEP * rden
    along = (-STEP) * s * rn
    return [scale * c[a] + along * g[a] for a in range(3)], rden, wpart


class Around:
    def __init__(self, plane, strip, planes, row, lane):
        self.plane, self.planes, self.lane = plane, planes, lane
        self.at, self.upper = pl.ds(row, SUB), pl.ds(row + 1, SUB)
        self.strip = strip
        self.s = strip[self.at, :]
        self.now = [plane(k)[self.at, :] for k in range(planes + 1)]

    def steps(self, k):
        x = self.now[k]
        return (
            self.now[k + 1] - x,
            self.plane(k)[self.upper, :] - x,
            col_after(x, self.s, k, self.lane) - x,
        )

    def strip_steps(self):
        x = self.s
        return turn(x, -GROUP) - x, self.strip[self.upper, :] - x, turn(x, -1) - x


class Back:
    def __init__(self, carried, lane):
        self.carried, self.lane = carried, lane
        self.top = lax.broadcasted_iota(jnp.int32, (SUB, LANES), 0) == 0
        self.last, self.out = None, []

    def row_before(self, x):
        down = pltpu.roll(x, 1, 0)
        before = jnp.where(self.top, self.carried[len(self.out)], down)
        self.out.append(down)
        return before

    def strip(self, cg):
        self.s = cg[2]
        x = cg[0] - jnp.where(self.lane // GROUP >= 2, turn(cg[0], GROUP), 0.0)
        x = x + (cg[1] - self.row_before(cg[1]))
        return x + (cg[2] - turn(cg[2], 1))

    def plane(self, k, cg):
        x = cg[0] if self.last is None else cg[0] - self.last
        self.last = cg[0]
        x = x + (cg[1] - self.row_before(cg[1]))
        return x + (cg[2] - col_before(cg[2], self.s, k, self.lane))


def over_tiles(tiles, planes, step):
    def body(t, carried):
        later = Later()
        carried = step(t, carried, later)
        later.flush()
        return tuple(carried)

    lax.fori_loop(0, tiles, body, (jnp.zeros((SUB, LANES), jnp.float32),) * (planes + 1))


def chooser(mid, first, ghost, planes):
    return lambda k: first if k == 0 else ghost if k == planes else mid.at[k]


def first_step(counts, em, full, v, vs, *refs):
    planes, rows = em.shape[1], em.shape[2] - 2 * PAD
    nz = phases(counts["gz"])
    got, refs = refs[:nz], refs[nz:]
    (r, rs, rd, rds, wp, top, tops), outs, scratch = refs[:7], refs[7 : 7 + nz], refs[7 + nz :]
    first, ghost, strip = scratch
    link, row_link, col_link = (Link(a, counts[a]) for a in ("gz", "gx", "gy"))
    lane = lane_ids()
    lost = jnp.logical_and(lax.rem(lane, GROUP) // 4 == 1, jnp.logical_not(col_link.after))
    tiles, flat, folded = sizes(rows)
    below, above = plane_in(link, got)
    settle(v.at[0, 0], vs.at[0], em.at[0, planes - 1], full.at[0], below, above, 0, link.after, first, ghost, strip, planes, rows)

    def step(t, carried, later):
        row = pl.multiple_of(SUB * t + SUB, SUB)
        at = pl.ds(row, SUB)
        keep = jnp.logical_or(t < tiles - 1, row_link.after)
        field = Around(chooser(v.at[0], first, ghost, planes), strip, planes, row, lane)
        back = Back(carried, lane)
        cg, rden, _ = pointwise(
            field.strip_steps(), [full[6 + a, at, :] for a in range(3)], [full[a, at, :] for a in range(3)], full[WEIGHT, at, :]
        )
        later.put(rds, (at, ALL), rden)
        later.put(tops, (at, ALL), cg[0])
        later.put(rs, (at, ALL), jnp.where(keep, jnp.where(lost, 0.0, back.strip(cg)), 0.0))
        for k in range(planes):
            cg, rden, wpart = pointwise(
                field.steps(k), [em[6 + a, k, at, :] for a in range(3)], [em[a, k, at, :] for a in range(3)], em[WEIGHT, k, at, :]
            )
            later.put(rd, (k, at, ALL), rden)
            later.put(wp, (k, at, ALL), wpart)
            later.put(r, (k, at, ALL), jnp.where(keep, back.plane(k, cg), 0.0))
            if k == planes - 1:
                later.put(top, (at, ALL), cg[0])
        return back.out

    over_tiles(tiles, planes, step)
    plane_out(link, outs, [(top, tops)], [(r.at[0], rs)], planes, rows)


def second_step(counts, em, full, v, vs, *refs):
    planes, rows = em.shape[1], em.shape[2] - 2 * PAD
    nz = phases(counts["gz"])
    got_v, refs = refs[:nz], refs[nz:]
    (r1, r1s, rd, rds, wp, top1, top1s), refs = refs[:7], refs[7:]
    got_r, refs = refs[:nz], refs[nz:]
    (x, r2, r2s, top, tops, wg, dg), outs, scratch = refs[:7], refs[7 : 7 + nz], refs[7 + nz :]
    first, ghost, strip, first_r, ghost_r, strip_r = scratch
    link, row_link, col_link = (Link(a, counts[a]) for a in ("gz", "gx", "gy"))
    lane = lane_ids()
    part = lax.rem(lane, GROUP) // 4
    lost = jnp.logical_and(part == 1, jnp.logical_not(col_link.after))
    outside = jnp.logical_and(part == 2, jnp.logical_not(col_link.before))
    tiles, flat, folded = sizes(rows)
    below, above = plane_in(link, got_v)
    settle(
        v.at[1, 0], vs.at[1], em.at[3, planes - 1], full.at[3], below, above, flat + folded, link.after, first, ghost, strip, planes, rows
    )
    below_r, above_r = plane_in(link, got_r)
    settle(r1.at[0], r1s, top1, top1s, below_r, above_r, 0, link.after, first_r, ghost_r, strip_r, planes, rows)

    def step(t, carried, later):
        row = pl.multiple_of(SUB * t + SUB, SUB)
        at = pl.ds(row, SUB)
        keep = jnp.logical_or(t < tiles - 1, row_link.after)
        inside = jnp.logical_or(t > 0, row_link.before)
        field = Around(chooser(v.at[1], first, ghost, planes), strip, planes, row, lane)
        spread = Around(chooser(r1, first_r, ghost_r, planes), strip_r, planes, row, lane)
        back = Back(carried, lane)
        rden = rds[at, :]
        down = spread.strip_steps()
        c = [jnp.where(inside, jnp.where(outside, 0.0, full[6 + a, at, :] * rden + down[a]), 0.0) for a in range(3)]
        cg, _, _ = pointwise(field.strip_steps(), c, [full[3 + a, at, :] for a in range(3)], full[WEIGHT, at, :])
        later.put(tops, (at, ALL), cg[0])
        later.put(r2s, (at, ALL), jnp.where(keep, jnp.where(lost, 0.0, back.strip(cg)), 0.0))
        for k in range(planes):
            rden = rd[k, at, :]
            down = spread.steps(k)
            c = [jnp.where(inside, em[6 + a, k, at, :] * rden + down[a], 0.0) for a in range(3)]
            cg, rden, wpart = pointwise(field.steps(k), c, [em[3 + a, k, at, :] for a in range(3)], em[WEIGHT, k, at, :])
            for a in range(3):
                later.put(x, (a, k, at, ALL), c[a] * rden)
            later.put(wg, (k, at, ALL), wp[k, at, :] + wpart)
            later.put(dg, (k, at, ALL), spread.now[k])
            later.put(r2, (k, at, ALL), jnp.where(keep, back.plane(k, cg), 0.0))
            if k == planes - 1:
                later.put(top, (at, ALL), cg[0])
        return back.out

    over_tiles(tiles, planes, step)
    plane_out(link, outs, [(top, tops)], [(r2.at[0], r2s)], planes, rows)


def finish(counts, x, r2, r2s, top, tops, wg, dg, *refs):
    planes, rows = r2.shape[0], r2.shape[1] - 2 * PAD
    nz = phases(counts["gz"])
    got, (grad, weight_grad, data_grad), scratch = refs[:nz], refs[nz : nz + 3], refs[nz + 3 :]
    first, ghost, strip = scratch
    link = Link("gz", counts["gz"])
    lane = lane_ids()
    below, above = plane_in(link, got)
    settle(r2.at[0], r2s, top, tops, below, above, 0, link.after, first, ghost, strip, planes, rows)

    @pl.loop(0, rows // SUB, unroll=2)
    def _(t):
        row = pl.multiple_of(SUB * t + PAD, SUB)
        at, to = pl.ds(row, SUB), pl.ds(pl.multiple_of(SUB * t, SUB), SUB)
        spread = Around(chooser(r2, first, ghost, planes), strip, planes, row, lane)
        later = Later()
        for k in range(planes):
            down = spread.steps(k)
            for a in range(3):
                later.put(grad, (a, k, to, ALL), x[a, k, at, :] + down[a])
            later.put(weight_grad, (k, to, ALL), wg[k, at, :])
            later.put(data_grad, (k, to, ALL), INVERSE * (dg[k, at, :] + spread.now[k]))
        later.flush()


def call(body, counts, operands, outs, scratch=(), space=pltpu.VMEM, grant=16):
    held = pl.BlockSpec(memory_space=pltpu.VMEM)
    return pl.pallas_call(
        functools.partial(body, counts),
        out_shape=outs,
        in_specs=[pl.BlockSpec(memory_space=space)] * len(operands),
        out_specs=[held] * len(outs),
        scratch_shapes=list(scratch),
        compiler_params=pltpu.CompilerParams(vmem_limit_bytes=grant * 1024 * 1024),
        name=body.__name__,
    )(*operands)


def vmem(*shape):
    return pltpu.VMEM(shape, jnp.float32)


def shards(counts, data, weight, dual_start, dual_mid, cotangent):
    planes, rows, cols = data.shape
    held = rows + 2 * PAD
    tiles, flat, folded = sizes(rows)
    nx, ny, nz = (phases(counts[a]) for a in ("gx", "gy", "gz"))
    raw = (dual_mid, dual_start, cotangent, weight, data)
    block, strip, line = vmem(planes, held, cols), vmem(held, LANES), vmem(held, cols)

    sent = call(
        rows_out,
        counts,
        raw,
        [vmem(planes * offsets()[1], cols)] * nx,
        [vmem(*x.shape[:-2], SUB, cols) for x in raw for _ in range(2)] + [pltpu.SemaphoreType.DMA((2 * len(raw),))],
        pltpu.HBM,
        60,
    )
    got = swap(sent, "gx", counts["gx"], "gy", counts["gy"])
    em, es, *sent = call(
        build, counts, (*raw, *got), [vmem(FIELDS, planes, held, cols), vmem(FIELDS, held, LANES)] + [vmem(2, flat, LANES)] * ny
    )
    got = swap(sent, "gy", counts["gy"], "gx", counts["gx"])
    one = flat + folded
    full, v, vs, *sent = call(
        strips_and_values,
        counts,
        (em, es, *got),
        [vmem(FIELDS, held, LANES), vmem(2, planes, held, cols), vmem(2, held, LANES)] + [vmem(2 * one, LANES)] * nz,
    )
    got_v = swap(sent, "gz", counts["gz"], "gy", counts["gy"])
    state = [block, strip, block, strip, block, line, strip]
    work = [line, line, strip]
    *first, = call(
        first_step,
        counts,
        (em, full, v, vs, *got_v),
        state + [vmem(one, LANES)] * nz,
        work,
    )
    got_r = swap(first[7:], "gz", counts["gz"], "gy", counts["gy"])
    *second, = call(
        second_step,
        counts,
        (em, full, v, vs, *got_v, *first[:7], *got_r),
        [vmem(3, planes, held, cols), block, strip, line, strip, block, block] + [vmem(one, LANES)] * nz,
        work + work,
    )
    got = swap(second[7:], "gz", counts["gz"], "gy", counts["gy"])
    out = jax.ShapeDtypeStruct
    return tuple(call(
        finish,
        counts,
        (*second[:7], *got),
        [out(dual_mid.shape, jnp.float32), out(data.shape, jnp.float32), out(data.shape, jnp.float32)],
        work,
    ))


def solution(mesh):
    field, dual = P("gz", "gx", "gy"), P(None, "gz", "gx", "gy")
    return jax.shard_map(
        functools.partial(shards, dict(mesh.shape)),
        mesh=mesh,
        in_specs=(field, field, dual, dual, dual),
        out_specs=(dual, field, field),
        check_vma=False,
    )
```

```python
import functools

import jax
import jax.numpy as jnp
from jax import lax
from jax.experimental import pallas as pl
from jax.experimental.pallas import tpu as pltpu
from jax.sharding import PartitionSpec as P

STEP = 0.08
INVERSE = 0.5
SMOOTH = 0.01

AFTER = (3, 3, 3, 2, 2, 2, 2, 2, 2, 2, 3)
BEFORE = (2, 3, 2, 1, 2, 1, 2, 2, 2, 2, 2)
FIELDS = len(AFTER)
WEIGHT, DATA = 9, 10
PAD = 16
SUB = 8
UNROLL = 3
TOGETHER = 3
LANES = 128
GROUP = 16


class Link:
    def __init__(self, axis, count):
        place = lax.axis_index(axis)
        self.even = lax.rem(place, 2) == 0
        self.odd = jnp.logical_not(self.even)
        self.before = place > 0
        self.after = place < count - 1


def phases(count):
    return 1 if count == 2 else 2


def swap(values, axis, count, spare, spare_count):
    out = [lax.all_gather(values[0], axis, axis_index_groups=[[i, i + 1] for i in range(0, count, 2)])]
    if count > 2:
        at = lambda i, j: i * spare_count + j
        groups = [[at(i, j), at(i + 1, j)] for i in range(1, count - 1, 2) for j in range(spare_count)]
        groups += [[at(i, j), at(i, j + 1)] for i in (0, count - 1) for j in range(0, spare_count, 2)]
        out.append(lax.all_gather(values[1], (axis, spare), axis_index_groups=groups))
    return out


def send(link, outs, up, down):
    @pl.when(link.even)
    def _():
        up(outs[0])
        if len(outs) > 1:
            down(outs[1])

    @pl.when(link.odd)
    def _():
        down(outs[0])
        if len(outs) > 1:
            up(outs[1])


def receive(link, ins, before, after):
    pl.when(link.odd)(lambda: before(ins[0].at[0]))
    pl.when(link.even)(lambda: after(ins[0].at[1]))
    if len(ins) > 1:
        pl.when(jnp.logical_and(link.even, link.before))(lambda: before(ins[1].at[0]))
        pl.when(jnp.logical_and(link.odd, link.after))(lambda: after(ins[1].at[1]))
    pl.when(jnp.logical_not(link.before))(lambda: before(None))
    pl.when(jnp.logical_not(link.after))(lambda: after(None))


class Later:
    def __init__(self):
        self.items = []

    def put(self, ref, index, value):
        self.items.append((ref, index, value))

    def flush(self):
        for ref, index, value in self.items:
            ref[index] = value


ALL = slice(None)


def batches(count, size):
    return [range(i, min(i + size, count)) for i in range(0, count, size)]


def lane_ids():
    return lax.broadcasted_iota(jnp.int32, (SUB, LANES), 1)


def turn(x, by):
    return pltpu.roll(x, by % LANES if isinstance(by, int) else lax.rem(by + 4 * LANES, LANES), 1)


def take(x, lanes):
    return jnp.take_along_axis(x, lanes, axis=1)


def col_before(x, strip, k, lane):
    return jnp.where(lane == 0, turn(strip, -(GROUP * (k + 1) + 11)), turn(x, 1))


def col_after(x, strip, k, lane):
    return jnp.where(lane == LANES - 1, turn(strip, LANES - 1 - (GROUP * (k + 1) + 4)), turn(x, -1))


def sources(dm, ds, ct, w, d):
    return [(r, a) for r in (dm, ds, ct) for a in range(3)] + [(w, None), (d, None)]


def src_rows(source, k, rows):
    ref, a = source
    return ref[k, rows, :] if a is None else ref[a, k, rows, :]


def offsets():
    out, total = [], 0
    for f in range(FIELDS):
        out.append(total)
        total += AFTER[f]
    return out, total


def rows_out(counts, *refs):
    nx = phases(counts["gx"])
    raw, whole, outs, (*edges, sems) = refs[:5], refs[5:7], refs[7 : 7 + nx], refs[7 + nx :]
    planes, rows = raw[4].shape[0], raw[4].shape[1]
    copies = []
    for i, ref in enumerate(raw):
        for end, at in enumerate((0, rows - SUB)):
            rows_at = pl.ds(at, SUB)
            view = ref.at[:, :, rows_at, :] if len(ref.shape) == 4 else ref.at[:, rows_at, :]
            copies.append(pltpu.make_async_copy(view, edges[2 * i + end], sems.at[2 * i + end]))
    late = [pltpu.make_async_copy(raw[3 + i], whole[i], sems.at[2 * len(raw) + i]) for i in range(2)]
    for copy in copies + late:
        copy.start()
    for copy in copies:
        copy.wait()
    head, tail = sources(*edges[0::2]), sources(*edges[1::2])
    offs, per = offsets()

    def up(out):
        for f in range(FIELDS):
            for k in range(planes):
                out[pl.ds(per * k + offs[f], BEFORE[f]), :] = src_rows(tail[f], k, pl.ds(SUB - BEFORE[f], BEFORE[f]))

    def down(out):
        for f in range(FIELDS):
            for k in range(planes):
                out[pl.ds(per * k + offs[f], AFTER[f]), :] = src_rows(head[f], k, pl.ds(0, AFTER[f]))

    send(Link("gx", counts["gx"]), outs, up, down)
    for copy in late:
        copy.wait()


def column_lanes(planes):
    firsts, total = [], 0
    for f in range(FIELDS):
        firsts.append(total)
        total += planes * AFTER[f]
    return firsts


def pack_lanes(lane, planes, up):
    out, firsts = jnp.zeros_like(lane), column_lanes(planes)
    for f in range(FIELDS):
        deep = AFTER[f]
        for k in range(planes):
            first = firsts[f] + k * deep
            at = GROUP * (k + 1) + jnp.where(up, 4 - deep, 12)
            out = jnp.where(lane >= first, lane - first + at, out)
    return jnp.minimum(out, LANES - 1)


def unpack_lanes(lane, planes, f):
    deep = AFTER[f]
    step = lax.rem(lane, 4)
    step = jnp.where(lax.rem(lane, GROUP) // 4 == 1, step, step - (4 - deep))
    plane = lane // GROUP - 1
    return jnp.clip(column_lanes(planes)[f] + plane * deep + step, 0, LANES - 1)


def build(counts, dm, ds, ct, w, d, *refs):
    planes, rows = d.shape[0], d.shape[1]
    nx, ny = phases(counts["gx"]), phases(counts["gy"])
    got, (em, es), outs = refs[:nx], refs[nx : nx + 2], refs[nx + 2 :]
    src = sources(dm, ds, ct, w, d)
    offs, per = offsets()
    lane = lane_ids()

    def halo(start, counted, deep):
        def fill(ref):
            for f in range(FIELDS):
                for k in range(planes):
                    if ref is None:
                        at, many = start(deep), deep
                        value = jnp.full((deep, LANES), 1.0 if f == WEIGHT else 0.0, jnp.float32)
                    else:
                        at, many = start(counted[f]), counted[f]
                        value = ref[pl.ds(per * k + offs[f], many), :]
                        value = 1.0 / value if f == WEIGHT else value
                    em[f, k, pl.ds(at, many), :] = value

        return fill

    receive(
        Link("gx", counts["gx"]),
        got,
        halo(lambda n: PAD - n, BEFORE, 3),
        halo(lambda n: PAD + rows, AFTER, 3),
    )
    link = Link("gy", counts["gy"])
    part = lax.rem(lane, GROUP) // 4
    plane_of = lane // GROUP
    own = jnp.logical_or(part == 0, part == 3)
    edges = lax.rem(lane, 4) + jnp.where(part == 0, LANES - 4, 0)
    packing = [pack_lanes(lane, planes, link.even if p == 0 else link.odd) for p in range(ny)]

    def tile(row, read, later):
        packed = [None] * ny
        for f in range(FIELDS):
            strip = jnp.full((SUB, LANES), 1.0 if f == WEIGHT else 0.0, jnp.float32)
            for k in range(planes):
                strip = jnp.where(jnp.logical_and(own, plane_of == k + 1), take(read(f, k), edges), strip)
            later.put(es, (f, pl.ds(row, SUB), ALL), strip)
            for p in range(ny):
                moved = take(strip, packing[p])
                packed[p] = moved if f == 0 else jnp.where(lane >= column_lanes(planes)[f], moved, packed[p])
        for p in range(ny):
            later.put(outs[p], (pl.ds(row - SUB, SUB), ALL), packed[p])

    @pl.loop(0, rows // SUB)
    def _(t):
        inside = pl.multiple_of(t * SUB, SUB)
        row = pl.multiple_of(t * SUB + PAD, SUB)

        later = Later()

        def read(f, k):
            x = src_rows(src[f], k, pl.ds(inside, SUB))
            x = 1.0 / x if f == WEIGHT else x
            em[f, k, pl.ds(row, SUB), :] = x
            return x

        tile(row, read, later)
        later.flush()

    @pl.loop(0, 2)
    def _(t):
        later = Later()
        row = pl.multiple_of(PAD - SUB + t * (rows + SUB), SUB)
        tile(row, lambda f, k: em[f, k, pl.ds(row, SUB), :], later)
        later.flush()


def fold(strip, group, out, base, tiles):
    group_of = lane_ids() // GROUP
    many = LANES // GROUP
    later = Later()
    for i, some in enumerate(batches(tiles, many)):
        x = None
        for t in some:
            y = turn(strip[pl.ds(SUB * t + SUB, SUB), :], GROUP * (t % many - group))
            x = y if x is None else jnp.where(group_of == t % many, y, x)
        later.put(out, (pl.ds(base + SUB * i, SUB), ALL), x)
    later.flush()


def unfold(read, base, t, group):
    many = LANES // GROUP
    return turn(read(base + SUB * (t // many)), GROUP * (group - t % many))


def sizes(rows):
    tiles = (rows + 2 * PAD - 2 * SUB) // SUB
    folded = SUB * pl.cdiv(tiles * GROUP, LANES)
    return tiles, SUB * tiles, folded


def copy_rows(src, out, base, tiles):
    for some in batches(tiles, 9):
        later = Later()
        for t in some:
            later.put(out, (pl.ds(base + SUB * t, SUB), ALL), src[pl.ds(SUB * t + SUB, SUB), :])
        later.flush()


def plane_out(link, outs, up, down, planes, rows):
    tiles, flat, folded = sizes(rows)

    def put(items, group):
        def write(out):
            for i, (plane, strip) in enumerate(items):
                base = i * (flat + folded)
                copy_rows(plane, out, base, tiles)
                fold(strip, group, out, base + flat, tiles)

        return write

    send(link, outs, put(up, planes), put(down, 1))


def plane_in(link, ins):
    def at(index, first, known):
        def read(row):
            x = ins[0][index, pl.ds(row, SUB), :]
            if len(ins) > 1:
                x = jnp.where(first, x, ins[1][index, pl.ds(row, SUB), :])
            return jnp.where(known, x, 0.0)

        return read

    return at(0, link.odd, link.before), at(1, link.even, link.after)


def strips_and_values(counts, em, es, *refs):
    planes, rows = em.shape[1], em.shape[2] - 2 * PAD
    ny = phases(counts["gy"])
    got, (full, v, vs), outs = refs[:ny], refs[ny : ny + 3], refs[ny + 3 :]
    link = Link("gy", counts["gy"])
    row_link = Link("gx", counts["gx"])
    lane = lane_ids()
    part = lax.rem(lane, GROUP) // 4
    near = jnp.logical_or(part == 1, part == 2)
    real_after = jnp.logical_and(part == 1, link.after)
    real_before = jnp.logical_and(part == 2, link.before)
    lanes = [unpack_lanes(lane, planes, f) for f in range(FIELDS)]
    if ny == 1:
        other = jnp.where(link.even, 1, 0)
        blocks = [(lambda at: got[0][other, at, :], jnp.logical_or(real_after, real_before))]
    else:
        blocks = [
            (lambda at: jnp.where(link.even, got[0][1, at, :], got[1][1, at, :]), real_after),
            (lambda at: jnp.where(link.odd, got[0][0, at, :], got[1][0, at, :]), real_before),
        ]
    lost = jnp.logical_and(part == 1, jnp.logical_not(link.after))
    inner = lane // GROUP >= 2
    tiles, flat, folded = sizes(rows)

    def strips(t, later):
        row = pl.multiple_of(SUB * t + SUB, SUB)
        at = pl.ds(pl.multiple_of(SUB * t, SUB), SUB)

        for f in range(FIELDS):
            x = jnp.where(near, 1.0 if f == WEIGHT else 0.0, es[f, pl.ds(row, SUB), :])
            for block, mask in blocks:
                x = jnp.where(mask, take(block(at), lanes[f]), x)
            later.put(full, (f, pl.ds(row, SUB), ALL), x)

    def values(t, later):
        row = pl.multiple_of(SUB * t + SUB, SUB)
        at, lower = pl.ds(row, SUB), pl.ds(row - 1, SUB)
        keep = jnp.logical_or(t < tiles - 1, row_link.after)
        for m in range(2):
            p0, p1, p2 = 3 * m, 3 * m + 1, 3 * m + 2
            s0, s2 = full[p0, at, :], full[p2, at, :]
            x = s0 - jnp.where(inner, turn(s0, GROUP), 0.0)
            x = x + (full[p1, at, :] - full[p1, lower, :])
            x = x + (s2 - turn(s2, 1))
            x = x - INVERSE * full[DATA, at, :]
            later.put(vs, (m, at, ALL), jnp.where(keep, jnp.where(lost, 0.0, x), 0.0))
            last = None
            for k in range(planes):
                x = now = em[p0, k, at, :]
                if k:
                    x = x - last
                last = now
                x = x + (em[p1, k, at, :] - em[p1, k, lower, :])
                y = em[p2, k, at, :]
                x = x + (y - col_before(y, s2, k, lane))
                x = x - INVERSE * em[DATA, k, at, :]
                later.put(v, (m, k, at, ALL), jnp.where(keep, x, 0.0))

    for body in (strips, values):

        @pl.loop(0, tiles // UNROLL)
        def _(t):
            later = Later()
            for u in range(UNROLL):
                body(t * UNROLL + u, later)
            later.flush()

    plane_out(
        Link("gz", counts["gz"]),
        outs,
        [(em.at[3 * m, planes - 1], full.at[3 * m]) for m in range(2)],
        [(v.at[m, 0], vs.at[m]) for m in range(2)],
        planes,
        rows,
    )


def settle(first, strip, last, last_strip, below, above, base, has_after, out_first, out_ghost, out_strip, planes, rows):
    tiles, flat, folded = sizes(rows)
    group = lane_ids() // GROUP
    for some in batches(tiles, 6):
        later = Later()
        for t in some:
            at = (pl.ds(SUB * t + SUB, SUB), ALL)
            sent = base + SUB * t
            later.put(out_first, at, first[at] - below(sent))
            later.put(out_ghost, at, jnp.where(has_after, above(sent) - last[at], 0.0))
            x = strip[at]
            x = jnp.where(group == 1, x - unfold(below, base + flat, t, 1), x)
            ghost = unfold(above, base + flat, t, planes + 1) - turn(last_strip[at], GROUP)
            ghost = jnp.where(has_after, ghost, 0.0)
            later.put(out_strip, at, jnp.where(group == planes + 1, ghost, x))
        later.flush()


def pointwise(g, c, p, rw):
    q = g[0] * g[0] + g[1] * g[1] + g[2] * g[2] + SMOOTH
    rn = lax.rsqrt(q)
    tn = STEP * (q * rn)
    rden = 1.0 / (1.0 + tn * rw)
    inner = c[0] * p[0] + c[1] * p[1] + c[2] * p[2]
    inner = inner + STEP * (c[0] * g[0] + c[1] * g[1] + c[2] * g[2])
    s = inner * rden * (rden * rw)
    wpart = s * (tn * rw)
    scale = STEP * rden
    along = (-STEP) * s * rn
    return [scale * c[a] + along * g[a] for a in range(3)], rden, wpart


class Around:
    def __init__(self, plane, strip, planes, row, lane):
        self.plane, self.planes, self.lane = plane, planes, lane
        self.at, self.upper = pl.ds(row, SUB), pl.ds(row + 1, SUB)
        self.strip = strip
        self.s = strip[self.at, :]
        self.now = [plane(k)[self.at, :] for k in range(planes + 1)]

    def steps(self, k):
        x = self.now[k]
        return (
            self.now[k + 1] - x,
            self.plane(k)[self.upper, :] - x,
            col_after(x, self.s, k, self.lane) - x,
        )

    def strip_steps(self):
        x = self.s
        return turn(x, -GROUP) - x, self.strip[self.upper, :] - x, turn(x, -1) - x


class Back:
    def __init__(self, carried, lane):
        self.carried, self.lane = carried, lane
        self.top = lax.broadcasted_iota(jnp.int32, (SUB, LANES), 0) == 0
        self.last, self.out = None, []

    def row_before(self, x):
        down = pltpu.roll(x, 1, 0)
        before = jnp.where(self.top, self.carried[len(self.out)], down)
        self.out.append(down)
        return before

    def strip(self, cg):
        self.s = cg[2]
        x = cg[0] - jnp.where(self.lane // GROUP >= 2, turn(cg[0], GROUP), 0.0)
        x = x + (cg[1] - self.row_before(cg[1]))
        return x + (cg[2] - turn(cg[2], 1))

    def plane(self, k, cg):
        x = cg[0] if self.last is None else cg[0] - self.last
        self.last = cg[0]
        x = x + (cg[1] - self.row_before(cg[1]))
        return x + (cg[2] - col_before(cg[2], self.s, k, self.lane))


def over_tiles(tiles, planes, step):
    def body(t, carried):
        later = Later()
        for u in range(TOGETHER):
            carried = step(t * TOGETHER + u, carried, later)
        later.flush()
        return tuple(carried)

    lax.fori_loop(0, tiles // TOGETHER, body, (jnp.zeros((SUB, LANES), jnp.float32),) * (planes + 1))


def chooser(mid, first, ghost, planes):
    return lambda k: first if k == 0 else ghost if k == planes else mid.at[k]


def first_step(counts, em, full, v, vs, *refs):
    planes, rows = em.shape[1], em.shape[2] - 2 * PAD
    nz = phases(counts["gz"])
    got, refs = refs[:nz], refs[nz:]
    (r, rs, rd, rds, wp, top, tops), outs, scratch = refs[:7], refs[7 : 7 + nz], refs[7 + nz :]
    first, ghost, strip = scratch
    link, row_link, col_link = (Link(a, counts[a]) for a in ("gz", "gx", "gy"))
    lane = lane_ids()
    lost = jnp.logical_and(lax.rem(lane, GROUP) // 4 == 1, jnp.logical_not(col_link.after))
    tiles, flat, folded = sizes(rows)
    below, above = plane_in(link, got)
    settle(v.at[0, 0], vs.at[0], em.at[0, planes - 1], full.at[0], below, above, 0, link.after, first, ghost, strip, planes, rows)

    def step(t, carried, later):
        row = pl.multiple_of(SUB * t + SUB, SUB)
        at = pl.ds(row, SUB)
        keep = jnp.logical_or(t < tiles - 1, row_link.after)
        field = Around(chooser(v.at[0], first, ghost, planes), strip, planes, row, lane)
        back = Back(carried, lane)
        cg, rden, _ = pointwise(
            field.strip_steps(), [full[6 + a, at, :] for a in range(3)], [full[a, at, :] for a in range(3)], full[WEIGHT, at, :]
        )
        later.put(rds, (at, ALL), rden)
        later.put(tops, (at, ALL), cg[0])
        later.put(rs, (at, ALL), jnp.where(keep, jnp.where(lost, 0.0, back.strip(cg)), 0.0))
        for k in range(planes):
            cg, rden, wpart = pointwise(
                field.steps(k), [em[6 + a, k, at, :] for a in range(3)], [em[a, k, at, :] for a in range(3)], em[WEIGHT, k, at, :]
            )
            later.put(rd, (k, at, ALL), rden)
            later.put(wp, (k, at, ALL), wpart)
            later.put(r, (k, at, ALL), jnp.where(keep, back.plane(k, cg), 0.0))
            if k == planes - 1:
                later.put(top, (at, ALL), cg[0])
        return back.out

    over_tiles(tiles, planes, step)
    plane_out(link, outs, [(top, tops)], [(r.at[0], rs)], planes, rows)


def second_step(counts, em, full, v, vs, *refs):
    planes, rows = em.shape[1], em.shape[2] - 2 * PAD
    nz = phases(counts["gz"])
    got_v, refs = refs[:nz], refs[nz:]
    (r1, r1s, rd, rds, wp, top1, top1s), refs = refs[:7], refs[7:]
    got_r, refs = refs[:nz], refs[nz:]
    (x, r2, r2s, top, tops, wg, dg), outs, scratch = refs[:7], refs[7 : 7 + nz], refs[7 + nz :]
    first, ghost, strip, first_r, ghost_r, strip_r = scratch
    link, row_link, col_link = (Link(a, counts[a]) for a in ("gz", "gx", "gy"))
    lane = lane_ids()
    part = lax.rem(lane, GROUP) // 4
    lost = jnp.logical_and(part == 1, jnp.logical_not(col_link.after))
    outside = jnp.logical_and(part == 2, jnp.logical_not(col_link.before))
    tiles, flat, folded = sizes(rows)
    below, above = plane_in(link, got_v)
    settle(
        v.at[1, 0], vs.at[1], em.at[3, planes - 1], full.at[3], below, above, flat + folded, link.after, first, ghost, strip, planes, rows
    )
    below_r, above_r = plane_in(link, got_r)
    settle(r1.at[0], r1s, top1, top1s, below_r, above_r, 0, link.after, first_r, ghost_r, strip_r, planes, rows)

    def step(t, carried, later):
        row = pl.multiple_of(SUB * t + SUB, SUB)
        at = pl.ds(row, SUB)
        keep = jnp.logical_or(t < tiles - 1, row_link.after)
        inside = jnp.logical_or(t > 0, row_link.before)
        field = Around(chooser(v.at[1], first, ghost, planes), strip, planes, row, lane)
        spread = Around(chooser(r1, first_r, ghost_r, planes), strip_r, planes, row, lane)
        back = Back(carried, lane)
        rden = rds[at, :]
        down = spread.strip_steps()
        c = [jnp.where(inside, jnp.where(outside, 0.0, full[6 + a, at, :] * rden + down[a]), 0.0) for a in range(3)]
        cg, _, _ = pointwise(field.strip_steps(), c, [full[3 + a, at, :] for a in range(3)], full[WEIGHT, at, :])
        later.put(tops, (at, ALL), cg[0])
        later.put(r2s, (at, ALL), jnp.where(keep, jnp.where(lost, 0.0, back.strip(cg)), 0.0))
        for k in range(planes):
            rden = rd[k, at, :]
            down = spread.steps(k)
            c = [jnp.where(inside, em[6 + a, k, at, :] * rden + down[a], 0.0) for a in range(3)]
            cg, rden, wpart = pointwise(field.steps(k), c, [em[3 + a, k, at, :] for a in range(3)], em[WEIGHT, k, at, :])
            for a in range(3):
                later.put(x, (a, k, at, ALL), c[a] * rden)
            later.put(wg, (k, at, ALL), wp[k, at, :] + wpart)
            later.put(dg, (k, at, ALL), spread.now[k])
            later.put(r2, (k, at, ALL), jnp.where(keep, back.plane(k, cg), 0.0))
            if k == planes - 1:
                later.put(top, (at, ALL), cg[0])
        return back.out

    over_tiles(tiles, planes, step)
    plane_out(link, outs, [(top, tops)], [(r2.at[0], r2s)], planes, rows)


def finish(counts, x, r2, r2s, top, tops, wg, dg, *refs):
    planes, rows = r2.shape[0], r2.shape[1] - 2 * PAD
    nz = phases(counts["gz"])
    got, (grad, weight_grad, data_grad), scratch = refs[:nz], refs[nz : nz + 3], refs[nz + 3 :]
    first, ghost, strip = scratch
    link = Link("gz", counts["gz"])
    lane = lane_ids()
    below, above = plane_in(link, got)
    settle(r2.at[0], r2s, top, tops, below, above, 0, link.after, first, ghost, strip, planes, rows)

    @pl.loop(0, rows // SUB, unroll=2)
    def _(t):
        row = pl.multiple_of(SUB * t + PAD, SUB)
        at, to = pl.ds(row, SUB), pl.ds(pl.multiple_of(SUB * t, SUB), SUB)
        spread = Around(chooser(r2, first, ghost, planes), strip, planes, row, lane)
        later = Later()
        for k in range(planes):
            down = spread.steps(k)
            for a in range(3):
                later.put(grad, (a, k, to, ALL), x[a, k, at, :] + down[a])
            later.put(weight_grad, (k, to, ALL), wg[k, at, :])
            later.put(data_grad, (k, to, ALL), INVERSE * (dg[k, at, :] + spread.now[k]))
        later.flush()


def call(body, counts, operands, outs, scratch=(), space=pltpu.VMEM, grant=16):
    held = pl.BlockSpec(memory_space=pltpu.VMEM)
    return pl.pallas_call(
        functools.partial(body, counts),
        out_shape=outs,
        in_specs=[pl.BlockSpec(memory_space=space)] * len(operands),
        out_specs=[held] * len(outs),
        scratch_shapes=list(scratch),
        compiler_params=pltpu.CompilerParams(vmem_limit_bytes=grant * 1024 * 1024),
        name=body.__name__,
    )(*operands)


def vmem(*shape):
    return pltpu.VMEM(shape, jnp.float32)


def shards(counts, data, weight, dual_start, dual_mid, cotangent):
    planes, rows, cols = data.shape
    held = rows + 2 * PAD
    tiles, flat, folded = sizes(rows)
    nx, ny, nz = (phases(counts[a]) for a in ("gx", "gy", "gz"))
    raw = (dual_mid, dual_start, cotangent, weight, data)
    block, strip, line = vmem(planes, held, cols), vmem(held, LANES), vmem(held, cols)

    near_weight, near_data, *sent = call(
        rows_out,
        counts,
        raw,
        [vmem(*data.shape)] * 2 + [vmem(planes * offsets()[1], cols)] * nx,
        [vmem(*x.shape[:-2], SUB, cols) for x in raw for _ in range(2)] + [pltpu.SemaphoreType.DMA((2 * len(raw) + 2,))],
        pltpu.HBM,
        60,
    )
    got = swap(sent, "gx", counts["gx"], "gy", counts["gy"])
    em, es, *sent = call(
        build, counts, (*raw[:3], near_weight, near_data, *got), [vmem(FIELDS, planes, held, cols), vmem(FIELDS, held, LANES)] + [vmem(flat, LANES)] * ny
    )
    got = swap(sent, "gy", counts["gy"], "gx", counts["gx"])
    one = flat + folded
    full, v, vs, *sent = call(
        strips_and_values,
        counts,
        (em, es, *got),
        [vmem(FIELDS, held, LANES), vmem(2, planes, held, cols), vmem(2, held, LANES)] + [vmem(2 * one, LANES)] * nz,
    )
    got_v = swap(sent, "gz", counts["gz"], "gy", counts["gy"])
    state = [block, strip, block, strip, block, line, strip]
    work = [line, line, strip]
    *first, = call(
        first_step,
        counts,
        (em, full, v, vs, *got_v),
        state + [vmem(one, LANES)] * nz,
        work,
    )
    got_r = swap(first[7:], "gz", counts["gz"], "gy", counts["gy"])
    *second, = call(
        second_step,
        counts,
        (em, full, v, vs, *got_v, *first[:7], *got_r),
        [vmem(3, planes, held, cols), block, strip, line, strip, block, block] + [vmem(one, LANES)] * nz,
        work + work,
    )
    got = swap(second[7:], "gz", counts["gz"], "gy", counts["gy"])
    out = jax.ShapeDtypeStruct
    return tuple(call(
        finish,
        counts,
        (*second[:7], *got),
        [out(dual_mid.shape, jnp.float32), out(data.shape, jnp.float32), out(data.shape, jnp.float32)],
        work,
    ))


def solution(mesh):
    field, dual = P("gz", "gx", "gy"), P(None, "gz", "gx", "gy")
    return jax.shard_map(
        functools.partial(shards, dict(mesh.shape)),
        mesh=mesh,
        in_specs=(field, field, dual, dual, dual),
        out_specs=(dual, field, field),
        check_vma=False,
    )
```

```python
import functools

import jax
import jax.numpy as jnp
from jax import lax
from jax.experimental import pallas as pl
from jax.experimental.pallas import tpu as pltpu
from jax.sharding import PartitionSpec as P

STEP = 0.08
INVERSE = 0.5
SMOOTH = 0.01

AFTER = (3, 3, 3, 2, 2, 2, 2, 2, 2, 2, 3)
BEFORE = (2, 3, 2, 1, 2, 1, 2, 2, 2, 2, 2)
FIELDS = len(AFTER)
WEIGHT, DATA = 9, 10
PAD = 16
SUB = 8
UNROLL = 18
TOGETHER = 6
PAIRED = 4
LAST = 16
LANES = 128
GROUP = 16


class Link:
    def __init__(self, axis, count):
        place = lax.axis_index(axis)
        self.even = lax.rem(place, 2) == 0
        self.odd = jnp.logical_not(self.even)
        self.before = place > 0
        self.after = place < count - 1


def phases(count):
    return 1 if count == 2 else 2


def swap(values, axis, count, spare, spare_count):
    out = [lax.all_gather(values[0], axis, axis_index_groups=[[i, i + 1] for i in range(0, count, 2)])]
    if count > 2:
        at = lambda i, j: i * spare_count + j
        groups = [[at(i, j), at(i + 1, j)] for i in range(1, count - 1, 2) for j in range(spare_count)]
        groups += [[at(i, j), at(i, j + 1)] for i in (0, count - 1) for j in range(0, spare_count, 2)]
        out.append(lax.all_gather(values[1], (axis, spare), axis_index_groups=groups))
    return out


def send(link, outs, up, down):
    @pl.when(link.even)
    def _():
        up(outs[0])
        if len(outs) > 1:
            down(outs[1])

    @pl.when(link.odd)
    def _():
        down(outs[0])
        if len(outs) > 1:
            up(outs[1])


def receive(link, ins, before, after):
    pl.when(link.odd)(lambda: before(ins[0].at[0]))
    pl.when(link.even)(lambda: after(ins[0].at[1]))
    if len(ins) > 1:
        pl.when(jnp.logical_and(link.even, link.before))(lambda: before(ins[1].at[0]))
        pl.when(jnp.logical_and(link.odd, link.after))(lambda: after(ins[1].at[1]))
    pl.when(jnp.logical_not(link.before))(lambda: before(None))
    pl.when(jnp.logical_not(link.after))(lambda: after(None))


class Later:
    def __init__(self):
        self.items = []

    def put(self, ref, index, value):
        self.items.append((ref, index, value))

    def flush(self):
        for ref, index, value in self.items:
            ref[index] = value


ALL = slice(None)


def in_groups(count, together, step):
    while count % together:
        together -= 1

    def body(t):
        later = Later()
        for u in range(together):
            step(t * together + u, later)
        later.flush()

    if together == count:
        body(0)
    else:
        pl.loop(0, count // together)(body)


def batches(count, size):
    return [range(i, min(i + size, count)) for i in range(0, count, size)]


def lane_ids():
    return lax.broadcasted_iota(jnp.int32, (SUB, LANES), 1)


def turn(x, by):
    return pltpu.roll(x, by % LANES if isinstance(by, int) else lax.rem(by + 4 * LANES, LANES), 1)


def take(x, lanes):
    return jnp.take_along_axis(x, lanes, axis=1)


def col_before(x, strip, k, lane):
    return jnp.where(lane == 0, turn(strip, -(GROUP * (k + 1) + 11)), turn(x, 1))


def col_after(x, strip, k, lane):
    return jnp.where(lane == LANES - 1, turn(strip, LANES - 1 - (GROUP * (k + 1) + 4)), turn(x, -1))


def sources(dm, ds, ct, w, d):
    return [(r, a) for r in (dm, ds, ct) for a in range(3)] + [(w, None), (d, None)]


def src_rows(source, k, rows):
    ref, a = source
    return ref[k, rows, :] if a is None else ref[a, k, rows, :]


def offsets():
    out, total = [], 0
    for f in range(FIELDS):
        out.append(total)
        total += AFTER[f]
    return out, total


def rows_out(counts, *refs):
    nx = phases(counts["gx"])
    raw, whole, outs, (*edges, sems) = refs[:5], refs[5:7], refs[7 : 7 + nx], refs[7 + nx :]
    planes, rows = raw[4].shape[0], raw[4].shape[1]
    copies = []
    for i, ref in enumerate(raw):
        for end, at in enumerate((0, rows - SUB)):
            rows_at = pl.ds(at, SUB)
            view = ref.at[:, :, rows_at, :] if len(ref.shape) == 4 else ref.at[:, rows_at, :]
            copies.append(pltpu.make_async_copy(view, edges[2 * i + end], sems.at[2 * i + end]))
    late = [pltpu.make_async_copy(raw[3 + i], whole[i], sems.at[2 * len(raw) + i]) for i in range(2)]
    for copy in copies + late:
        copy.start()
    for copy in copies:
        copy.wait()
    head, tail = sources(*edges[0::2]), sources(*edges[1::2])
    offs, per = offsets()

    def up(out):
        for f in range(FIELDS):
            for k in range(planes):
                out[pl.ds(per * k + offs[f], BEFORE[f]), :] = src_rows(tail[f], k, pl.ds(SUB - BEFORE[f], BEFORE[f]))

    def down(out):
        for f in range(FIELDS):
            for k in range(planes):
                out[pl.ds(per * k + offs[f], AFTER[f]), :] = src_rows(head[f], k, pl.ds(0, AFTER[f]))

    send(Link("gx", counts["gx"]), outs, up, down)
    for copy in late:
        copy.wait()


def column_lanes(planes):
    firsts, total = [], 0
    for f in range(FIELDS):
        firsts.append(total)
        total += planes * AFTER[f]
    return firsts


def pack_lanes(lane, planes, up):
    out, firsts = jnp.zeros_like(lane), column_lanes(planes)
    for f in range(FIELDS):
        deep = AFTER[f]
        for k in range(planes):
            first = firsts[f] + k * deep
            at = GROUP * (k + 1) + jnp.where(up, 4 - deep, 12)
            out = jnp.where(lane >= first, lane - first + at, out)
    return jnp.minimum(out, LANES - 1)


def unpack_lanes(lane, planes, f):
    deep = AFTER[f]
    step = lax.rem(lane, 4)
    step = jnp.where(lax.rem(lane, GROUP) // 4 == 1, step, step - (4 - deep))
    plane = lane // GROUP - 1
    return jnp.clip(column_lanes(planes)[f] + plane * deep + step, 0, LANES - 1)


def build(counts, dm, ds, ct, w, d, *refs):
    planes, rows = d.shape[0], d.shape[1]
    nx, ny = phases(counts["gx"]), phases(counts["gy"])
    got, (em, es), outs = refs[:nx], refs[nx : nx + 2], refs[nx + 2 :]
    src = sources(dm, ds, ct, w, d)
    offs, per = offsets()
    lane = lane_ids()

    def halo(start, counted, deep):
        def fill(ref):
            for f in range(FIELDS):
                for k in range(planes):
                    if ref is None:
                        at, many = start(deep), deep
                        value = jnp.full((deep, LANES), 1.0 if f == WEIGHT else 0.0, jnp.float32)
                    else:
                        at, many = start(counted[f]), counted[f]
                        value = ref[pl.ds(per * k + offs[f], many), :]
                        value = 1.0 / value if f == WEIGHT else value
                    em[f, k, pl.ds(at, many), :] = value

        return fill

    receive(
        Link("gx", counts["gx"]),
        got,
        halo(lambda n: PAD - n, BEFORE, 3),
        halo(lambda n: PAD + rows, AFTER, 3),
    )
    link = Link("gy", counts["gy"])
    part = lax.rem(lane, GROUP) // 4
    plane_of = lane // GROUP
    own = jnp.logical_or(part == 0, part == 3)
    edges = lax.rem(lane, 4) + jnp.where(part == 0, LANES - 4, 0)
    packing = [pack_lanes(lane, planes, link.even if p == 0 else link.odd) for p in range(ny)]

    def tile(row, read, later):
        for f in range(FIELDS):
            strip = jnp.full((SUB, LANES), 1.0 if f == WEIGHT else 0.0, jnp.float32)
            for k in range(planes):
                strip = jnp.where(jnp.logical_and(own, plane_of == k + 1), take(read(f, k), edges), strip)
            later.put(es, (f, pl.ds(row, SUB), ALL), strip)

    def pack(t, later):
        row = pl.multiple_of(t * SUB, SUB)
        for p in range(ny):
            out = take(es[0, pl.ds(row + SUB, SUB), :], packing[p])
            for f in range(1, FIELDS):
                moved = take(es[f, pl.ds(row + SUB, SUB), :], packing[p])
                out = jnp.where(lane >= column_lanes(planes)[f], moved, out)
            later.put(outs[p], (pl.ds(row, SUB), ALL), out)

    def inner(t, later):
        inside = pl.multiple_of(t * SUB, SUB)
        row = pl.multiple_of(t * SUB + PAD, SUB)

        def read(f, k):
            x = src_rows(src[f], k, pl.ds(inside, SUB))
            x = 1.0 / x if f == WEIGHT else x
            em[f, k, pl.ds(row, SUB), :] = x
            return x

        tile(row, read, later)

    def halos(t, later):
        for row in (PAD - SUB, PAD + rows):
            tile(row, lambda f, k: em[f, k, pl.ds(row, SUB), :], later)

    in_groups(rows // SUB, PAIRED, inner)
    in_groups(1, 1, halos)
    in_groups(sizes(rows)[0], UNROLL, pack)


def fold(strip, group, out, base, tiles):
    group_of = lane_ids() // GROUP
    many = LANES // GROUP
    later = Later()
    for i, some in enumerate(batches(tiles, many)):
        x = None
        for t in some:
            y = turn(strip[pl.ds(SUB * t + SUB, SUB), :], GROUP * (t % many - group))
            x = y if x is None else jnp.where(group_of == t % many, y, x)
        later.put(out, (pl.ds(base + SUB * i, SUB), ALL), x)
    later.flush()


def unfold(read, base, t, group):
    many = LANES // GROUP
    return turn(read(base + SUB * (t // many)), GROUP * (group - t % many))


def sizes(rows):
    tiles = (rows + 2 * PAD - 2 * SUB) // SUB
    folded = SUB * pl.cdiv(tiles * GROUP, LANES)
    return tiles, SUB * tiles, folded


def copy_rows(src, out, base, tiles):
    for some in batches(tiles, 9):
        later = Later()
        for t in some:
            later.put(out, (pl.ds(base + SUB * t, SUB), ALL), src[pl.ds(SUB * t + SUB, SUB), :])
        later.flush()


def plane_out(link, outs, up, down, planes, rows):
    tiles, flat, folded = sizes(rows)

    def put(items, group):
        def write(out):
            for i, (plane, strip) in enumerate(items):
                base = i * (flat + folded)
                copy_rows(plane, out, base, tiles)
                fold(strip, group, out, base + flat, tiles)

        return write

    send(link, outs, put(up, planes), put(down, 1))


def plane_in(link, ins):
    def at(index, first, known):
        def read(row):
            x = ins[0][index, pl.ds(row, SUB), :]
            if len(ins) > 1:
                x = jnp.where(first, x, ins[1][index, pl.ds(row, SUB), :])
            return jnp.where(known, x, 0.0)

        return read

    return at(0, link.odd, link.before), at(1, link.even, link.after)


def strips_and_values(counts, em, es, *refs):
    planes, rows = em.shape[1], em.shape[2] - 2 * PAD
    ny = phases(counts["gy"])
    got, (full, v, vs), outs = refs[:ny], refs[ny : ny + 3], refs[ny + 3 :]
    link = Link("gy", counts["gy"])
    row_link = Link("gx", counts["gx"])
    lane = lane_ids()
    part = lax.rem(lane, GROUP) // 4
    near = jnp.logical_or(part == 1, part == 2)
    real_after = jnp.logical_and(part == 1, link.after)
    real_before = jnp.logical_and(part == 2, link.before)
    lanes = [unpack_lanes(lane, planes, f) for f in range(FIELDS)]
    if ny == 1:
        other = jnp.where(link.even, 1, 0)
        blocks = [(lambda at: got[0][other, at, :], jnp.logical_or(real_after, real_before))]
    else:
        blocks = [
            (lambda at: jnp.where(link.even, got[0][1, at, :], got[1][1, at, :]), real_after),
            (lambda at: jnp.where(link.odd, got[0][0, at, :], got[1][0, at, :]), real_before),
        ]
    lost = jnp.logical_and(part == 1, jnp.logical_not(link.after))
    inner = lane // GROUP >= 2
    tiles, flat, folded = sizes(rows)

    def strips(t, later):
        row = pl.multiple_of(SUB * t + SUB, SUB)
        at = pl.ds(pl.multiple_of(SUB * t, SUB), SUB)

        for f in range(FIELDS):
            x = jnp.where(near, 1.0 if f == WEIGHT else 0.0, es[f, pl.ds(row, SUB), :])
            for block, mask in blocks:
                x = jnp.where(mask, take(block(at), lanes[f]), x)
            later.put(full, (f, pl.ds(row, SUB), ALL), x)

    def values(t, later):
        row = pl.multiple_of(SUB * t + SUB, SUB)
        at, lower = pl.ds(row, SUB), pl.ds(row - 1, SUB)
        keep = jnp.logical_or(t < tiles - 1, row_link.after)
        for m in range(2):
            p0, p1, p2 = 3 * m, 3 * m + 1, 3 * m + 2
            s0, s2 = full[p0, at, :], full[p2, at, :]
            x = s0 - jnp.where(inner, turn(s0, GROUP), 0.0)
            x = x + (full[p1, at, :] - full[p1, lower, :])
            x = x + (s2 - turn(s2, 1))
            x = x - INVERSE * full[DATA, at, :]
            later.put(vs, (m, at, ALL), jnp.where(keep, jnp.where(lost, 0.0, x), 0.0))
            last = None
            for k in range(planes):
                x = now = em[p0, k, at, :]
                if k:
                    x = x - last
                last = now
                x = x + (em[p1, k, at, :] - em[p1, k, lower, :])
                y = em[p2, k, at, :]
                x = x + (y - col_before(y, s2, k, lane))
                x = x - INVERSE * em[DATA, k, at, :]
                later.put(v, (m, k, at, ALL), jnp.where(keep, x, 0.0))

    in_groups(tiles, UNROLL, strips)
    in_groups(tiles, UNROLL, values)
    plane_out(
        Link("gz", counts["gz"]),
        outs,
        [(em.at[3 * m, planes - 1], full.at[3 * m]) for m in range(2)],
        [(v.at[m, 0], vs.at[m]) for m in range(2)],
        planes,
        rows,
    )


def settle(first, strip, last, last_strip, below, above, base, has_after, out_first, out_ghost, out_strip, planes, rows):
    tiles, flat, folded = sizes(rows)
    group = lane_ids() // GROUP
    for some in batches(tiles, 6):
        later = Later()
        for t in some:
            at = (pl.ds(SUB * t + SUB, SUB), ALL)
            sent = base + SUB * t
            later.put(out_first, at, first[at] - below(sent))
            later.put(out_ghost, at, jnp.where(has_after, above(sent) - last[at], 0.0))
            x = strip[at]
            x = jnp.where(group == 1, x - unfold(below, base + flat, t, 1), x)
            ghost = unfold(above, base + flat, t, planes + 1) - turn(last_strip[at], GROUP)
            ghost = jnp.where(has_after, ghost, 0.0)
            later.put(out_strip, at, jnp.where(group == planes + 1, ghost, x))
        later.flush()


def pointwise(g, c, p, rw):
    q = g[0] * g[0] + g[1] * g[1] + g[2] * g[2] + SMOOTH
    rn = lax.rsqrt(q)
    tn = STEP * (q * rn)
    rden = 1.0 / (1.0 + tn * rw)
    inner = c[0] * p[0] + c[1] * p[1] + c[2] * p[2]
    inner = inner + STEP * (c[0] * g[0] + c[1] * g[1] + c[2] * g[2])
    s = inner * rden * (rden * rw)
    wpart = s * (tn * rw)
    scale = STEP * rden
    along = (-STEP) * s * rn
    return [scale * c[a] + along * g[a] for a in range(3)], rden, wpart


class Around:
    def __init__(self, plane, strip, planes, row, lane):
        self.plane, self.planes, self.lane = plane, planes, lane
        self.at, self.upper = pl.ds(row, SUB), pl.ds(row + 1, SUB)
        self.strip = strip
        self.s = strip[self.at, :]
        self.now = [plane(k)[self.at, :] for k in range(planes + 1)]

    def steps(self, k):
        x = self.now[k]
        return (
            self.now[k + 1] - x,
            self.plane(k)[self.upper, :] - x,
            col_after(x, self.s, k, self.lane) - x,
        )

    def strip_steps(self):
        x = self.s
        return turn(x, -GROUP) - x, self.strip[self.upper, :] - x, turn(x, -1) - x


class Back:
    def __init__(self, carried, lane):
        self.carried, self.lane = carried, lane
        self.top = lax.broadcasted_iota(jnp.int32, (SUB, LANES), 0) == 0
        self.last, self.out = None, []

    def row_before(self, x):
        down = pltpu.roll(x, 1, 0)
        before = jnp.where(self.top, self.carried[len(self.out)], down)
        self.out.append(down)
        return before

    def strip(self, cg):
        self.s = cg[2]
        x = cg[0] - jnp.where(self.lane // GROUP >= 2, turn(cg[0], GROUP), 0.0)
        x = x + (cg[1] - self.row_before(cg[1]))
        return x + (cg[2] - turn(cg[2], 1))

    def plane(self, k, cg):
        x = cg[0] if self.last is None else cg[0] - self.last
        self.last = cg[0]
        x = x + (cg[1] - self.row_before(cg[1]))
        return x + (cg[2] - col_before(cg[2], self.s, k, self.lane))


def over_tiles(tiles, planes, step):
    together = TOGETHER
    while tiles % together:
        together -= 1

    def body(t, carried):
        later = Later()
        for u in range(together):
            carried = step(t * together + u, carried, later)
        later.flush()
        return tuple(carried)

    lax.fori_loop(0, tiles // together, body, (jnp.zeros((SUB, LANES), jnp.float32),) * (planes + 1))


def chooser(mid, first, ghost, planes):
    return lambda k: first if k == 0 else ghost if k == planes else mid.at[k]


def first_step(counts, em, full, v, vs, *refs):
    planes, rows = em.shape[1], em.shape[2] - 2 * PAD
    nz = phases(counts["gz"])
    got, refs = refs[:nz], refs[nz:]
    (r, rs, rd, rds, wp, top, tops), outs, scratch = refs[:7], refs[7 : 7 + nz], refs[7 + nz :]
    first, ghost, strip = scratch
    link, row_link, col_link = (Link(a, counts[a]) for a in ("gz", "gx", "gy"))
    lane = lane_ids()
    lost = jnp.logical_and(lax.rem(lane, GROUP) // 4 == 1, jnp.logical_not(col_link.after))
    tiles, flat, folded = sizes(rows)
    below, above = plane_in(link, got)
    settle(v.at[0, 0], vs.at[0], em.at[0, planes - 1], full.at[0], below, above, 0, link.after, first, ghost, strip, planes, rows)

    def step(t, carried, later):
        row = pl.multiple_of(SUB * t + SUB, SUB)
        at = pl.ds(row, SUB)
        keep = jnp.logical_or(t < tiles - 1, row_link.after)
        field = Around(chooser(v.at[0], first, ghost, planes), strip, planes, row, lane)
        back = Back(carried, lane)
        cg, rden, _ = pointwise(
            field.strip_steps(), [full[6 + a, at, :] for a in range(3)], [full[a, at, :] for a in range(3)], full[WEIGHT, at, :]
        )
        later.put(rds, (at, ALL), rden)
        later.put(tops, (at, ALL), cg[0])
        later.put(rs, (at, ALL), jnp.where(keep, jnp.where(lost, 0.0, back.strip(cg)), 0.0))
        for k in range(planes):
            cg, rden, wpart = pointwise(
                field.steps(k), [em[6 + a, k, at, :] for a in range(3)], [em[a, k, at, :] for a in range(3)], em[WEIGHT, k, at, :]
            )
            later.put(rd, (k, at, ALL), rden)
            later.put(wp, (k, at, ALL), wpart)
            later.put(r, (k, at, ALL), jnp.where(keep, back.plane(k, cg), 0.0))
            if k == planes - 1:
                later.put(top, (at, ALL), cg[0])
        return back.out

    over_tiles(tiles, planes, step)
    plane_out(link, outs, [(top, tops)], [(r.at[0], rs)], planes, rows)


def second_step(counts, em, full, v, vs, *refs):
    planes, rows = em.shape[1], em.shape[2] - 2 * PAD
    nz = phases(counts["gz"])
    got_v, refs = refs[:nz], refs[nz:]
    (r1, r1s, rd, rds, wp, top1, top1s), refs = refs[:7], refs[7:]
    got_r, refs = refs[:nz], refs[nz:]
    (x, r2, r2s, top, tops, wg, dg), outs, scratch = refs[:7], refs[7 : 7 + nz], refs[7 + nz :]
    first, ghost, strip, first_r, ghost_r, strip_r = scratch
    link, row_link, col_link = (Link(a, counts[a]) for a in ("gz", "gx", "gy"))
    lane = lane_ids()
    part = lax.rem(lane, GROUP) // 4
    lost = jnp.logical_and(part == 1, jnp.logical_not(col_link.after))
    outside = jnp.logical_and(part == 2, jnp.logical_not(col_link.before))
    tiles, flat, folded = sizes(rows)
    below, above = plane_in(link, got_v)
    settle(
        v.at[1, 0], vs.at[1], em.at[3, planes - 1], full.at[3], below, above, flat + folded, link.after, first, ghost, strip, planes, rows
    )
    below_r, above_r = plane_in(link, got_r)
    settle(r1.at[0], r1s, top1, top1s, below_r, above_r, 0, link.after, first_r, ghost_r, strip_r, planes, rows)

    def step(t, carried, later):
        row = pl.multiple_of(SUB * t + SUB, SUB)
        at = pl.ds(row, SUB)
        keep = jnp.logical_or(t < tiles - 1, row_link.after)
        inside = jnp.logical_or(t > 0, row_link.before)
        field = Around(chooser(v.at[1], first, ghost, planes), strip, planes, row, lane)
        spread = Around(chooser(r1, first_r, ghost_r, planes), strip_r, planes, row, lane)
        back = Back(carried, lane)
        rden = rds[at, :]
        down = spread.strip_steps()
        c = [jnp.where(inside, jnp.where(outside, 0.0, full[6 + a, at, :] * rden + down[a]), 0.0) for a in range(3)]
        cg, _, _ = pointwise(field.strip_steps(), c, [full[3 + a, at, :] for a in range(3)], full[WEIGHT, at, :])
        later.put(tops, (at, ALL), cg[0])
        later.put(r2s, (at, ALL), jnp.where(keep, jnp.where(lost, 0.0, back.strip(cg)), 0.0))
        for k in range(planes):
            rden = rd[k, at, :]
            down = spread.steps(k)
            c = [jnp.where(inside, em[6 + a, k, at, :] * rden + down[a], 0.0) for a in range(3)]
            cg, rden, wpart = pointwise(field.steps(k), c, [em[3 + a, k, at, :] for a in range(3)], em[WEIGHT, k, at, :])
            for a in range(3):
                later.put(x, (a, k, at, ALL), c[a] * rden)
            later.put(wg, (k, at, ALL), wp[k, at, :] + wpart)
            later.put(dg, (k, at, ALL), spread.now[k])
            later.put(r2, (k, at, ALL), jnp.where(keep, back.plane(k, cg), 0.0))
            if k == planes - 1:
                later.put(top, (at, ALL), cg[0])
        return back.out

    over_tiles(tiles, planes, step)
    plane_out(link, outs, [(top, tops)], [(r2.at[0], r2s)], planes, rows)


def finish(counts, x, r2, r2s, top, tops, wg, dg, *refs):
    planes, rows = r2.shape[0], r2.shape[1] - 2 * PAD
    nz = phases(counts["gz"])
    got, (grad, weight_grad, data_grad), scratch = refs[:nz], refs[nz : nz + 3], refs[nz + 3 :]
    first, ghost, strip = scratch
    link = Link("gz", counts["gz"])
    lane = lane_ids()
    below, above = plane_in(link, got)
    settle(r2.at[0], r2s, top, tops, below, above, 0, link.after, first, ghost, strip, planes, rows)

    def step(t, later):
        row = pl.multiple_of(SUB * t + PAD, SUB)
        at, to = pl.ds(row, SUB), pl.ds(pl.multiple_of(SUB * t, SUB), SUB)
        spread = Around(chooser(r2, first, ghost, planes), strip, planes, row, lane)
        for k in range(planes):
            down = spread.steps(k)
            for a in range(3):
                later.put(grad, (a, k, to, ALL), x[a, k, at, :] + down[a])
            later.put(weight_grad, (k, to, ALL), wg[k, at, :])
            later.put(data_grad, (k, to, ALL), INVERSE * (dg[k, at, :] + spread.now[k]))

    in_groups(rows // SUB, LAST, step)


def call(body, counts, operands, outs, scratch=(), space=pltpu.VMEM, grant=16):
    held = pl.BlockSpec(memory_space=pltpu.VMEM)
    return pl.pallas_call(
        functools.partial(body, counts),
        out_shape=outs,
        in_specs=[pl.BlockSpec(memory_space=space)] * len(operands),
        out_specs=[held] * len(outs),
        scratch_shapes=list(scratch),
        compiler_params=pltpu.CompilerParams(vmem_limit_bytes=grant * 1024 * 1024),
        name=body.__name__,
    )(*operands)


def vmem(*shape):
    return pltpu.VMEM(shape, jnp.float32)


def shards(counts, data, weight, dual_start, dual_mid, cotangent):
    planes, rows, cols = data.shape
    held = rows + 2 * PAD
    tiles, flat, folded = sizes(rows)
    nx, ny, nz = (phases(counts[a]) for a in ("gx", "gy", "gz"))
    raw = (dual_mid, dual_start, cotangent, weight, data)
    block, strip, line = vmem(planes, held, cols), vmem(held, LANES), vmem(held, cols)

    near_weight, near_data, *sent = call(
        rows_out,
        counts,
        raw,
        [vmem(*data.shape)] * 2 + [vmem(planes * offsets()[1], cols)] * nx,
        [vmem(*x.shape[:-2], SUB, cols) for x in raw for _ in range(2)] + [pltpu.SemaphoreType.DMA((2 * len(raw) + 2,))],
        pltpu.HBM,
        60,
    )
    got = swap(sent, "gx", counts["gx"], "gy", counts["gy"])
    em, es, *sent = call(
        build, counts, (*raw[:3], near_weight, near_data, *got), [vmem(FIELDS, planes, held, cols), vmem(FIELDS, held, LANES)] + [vmem(flat, LANES)] * ny
    )
    got = swap(sent, "gy", counts["gy"], "gx", counts["gx"])
    one = flat + folded
    full, v, vs, *sent = call(
        strips_and_values,
        counts,
        (em, es, *got),
        [vmem(FIELDS, held, LANES), vmem(2, planes, held, cols), vmem(2, held, LANES)] + [vmem(2 * one, LANES)] * nz,
    )
    got_v = swap(sent, "gz", counts["gz"], "gy", counts["gy"])
    state = [block, strip, block, strip, block, line, strip]
    work = [line, line, strip]
    *first, = call(
        first_step,
        counts,
        (em, full, v, vs, *got_v),
        state + [vmem(one, LANES)] * nz,
        work,
    )
    got_r = swap(first[7:], "gz", counts["gz"], "gy", counts["gy"])
    *second, = call(
        second_step,
        counts,
        (em, full, v, vs, *got_v, *first[:7], *got_r),
        [vmem(3, planes, held, cols), block, strip, line, strip, block, block] + [vmem(one, LANES)] * nz,
        work + work,
    )
    got = swap(second[7:], "gz", counts["gz"], "gy", counts["gy"])
    out = jax.ShapeDtypeStruct
    return tuple(call(
        finish,
        counts,
        (*second[:7], *got),
        [out(dual_mid.shape, jnp.float32), out(data.shape, jnp.float32), out(data.shape, jnp.float32)],
        work,
    ))


def solution(mesh):
    field, dual = P("gz", "gx", "gy"), P(None, "gz", "gx", "gy")
    return jax.shard_map(
        functools.partial(shards, dict(mesh.shape)),
        mesh=mesh,
        in_specs=(field, field, dual, dual, dual),
        out_specs=(dual, field, field),
        check_vma=False,
    )
```

```python
import functools

import jax
import jax.numpy as jnp
from jax import lax
from jax.experimental import pallas as pl
from jax.experimental.pallas import tpu as pltpu
from jax.sharding import PartitionSpec as P


STEP = 0.08
INVERSE = 0.5
SMOOTH = 0.01

AFTER = (3, 3, 3, 2, 2, 2, 2, 2, 2, 2, 3)
BEFORE = (2, 3, 2, 1, 2, 1, 2, 2, 2, 2, 2)
FIELDS = len(AFTER)
WEIGHT, DATA = 9, 10
PAD = 16
SUB = 8
UNROLL = 18
TOGETHER = 6
PAIRED = 4
LAST = 16
LANES = 128
GROUP = 16


class Link:
    def __init__(self, axis, count):
        place = lax.axis_index(axis)
        self.even = lax.rem(place, 2) == 0
        self.odd = jnp.logical_not(self.even)
        self.before = place > 0
        self.after = place < count - 1


def phases(count):
    return 1 if count == 2 else 2


def swap(values, axis, counts):
    spare = "gx" if axis == "gy" else "gy"
    names = tuple(n for n in counts if n in (axis, spare))
    count, wide = counts[axis], counts[spare]

    def place(i, j):
        return i * wide + j if names[0] == axis else j * count + i

    pairs = [[(place(i, j), place(i + 1, j)) for i in range(0, count, 2) for j in range(wide)]]
    if count > 2:
        pairs.append([(place(i, j), place(i + 1, j)) for i in range(1, count - 1, 2) for j in range(wide)])
        pairs[1] += [(place(i, j), place(i, j + 1)) for i in (0, count - 1) for j in range(0, wide, 2)]
    return [lax.ppermute(x, names, [q for a, b in some for q in ((a, b), (b, a))]) for x, some in zip(values, pairs)]


def send(link, outs, up, down):
    @pl.when(link.even)
    def _():
        up(outs[0])
        if len(outs) > 1:
            down(outs[1])

    @pl.when(link.odd)
    def _():
        down(outs[0])
        if len(outs) > 1:
            up(outs[1])


def receive(link, ins, before, after):
    pl.when(link.odd)(lambda: before(ins[0]))
    pl.when(link.even)(lambda: after(ins[0]))
    if len(ins) > 1:
        pl.when(jnp.logical_and(link.even, link.before))(lambda: before(ins[1]))
        pl.when(jnp.logical_and(link.odd, link.after))(lambda: after(ins[1]))
    pl.when(jnp.logical_not(link.before))(lambda: before(None))
    pl.when(jnp.logical_not(link.after))(lambda: after(None))


class Later:
    def __init__(self):
        self.items = []

    def put(self, ref, index, value):
        self.items.append((ref, index, value))

    def flush(self):
        for ref, index, value in self.items:
            ref[index] = value


ALL = slice(None)


def in_groups(count, together, step):
    while count % together:
        together -= 1

    def body(t):
        later = Later()
        for u in range(together):
            step(t * together + u, later)
        later.flush()

    if together == count:
        body(0)
    else:
        pl.loop(0, count // together)(body)


def batches(count, size):
    return [range(i, min(i + size, count)) for i in range(0, count, size)]


def lane_ids():
    return lax.broadcasted_iota(jnp.int32, (SUB, LANES), 1)


def turn(x, by):
    return pltpu.roll(x, by % LANES if isinstance(by, int) else lax.rem(by + 4 * LANES, LANES), 1)


def take(x, lanes):
    return jnp.take_along_axis(x, lanes, axis=1)


def col_before(x, strip, k, lane):
    return jnp.where(lane == 0, turn(strip, -(GROUP * (k + 1) + 11)), turn(x, 1))


def col_after(x, strip, k, lane):
    return jnp.where(lane == LANES - 1, turn(strip, LANES - 1 - (GROUP * (k + 1) + 4)), turn(x, -1))


def sources(dm, ds, ct, w, d):
    return [(r, a) for r in (dm, ds, ct) for a in range(3)] + [(w, None), (d, None)]


def src_rows(source, k, rows):
    ref, a = source
    return ref[k, rows, :] if a is None else ref[a, k, rows, :]


def offsets():
    out, total = [], 0
    for f in range(FIELDS):
        out.append(total)
        total += AFTER[f]
    return out, total


def rows_out(counts, *refs):
    nx = phases(counts["gx"])
    raw, whole, outs, (*edges, sems) = refs[:5], refs[5:7], refs[7 : 7 + nx], refs[7 + nx :]
    planes, rows = raw[4].shape[0], raw[4].shape[1]
    copies = []
    for i, ref in enumerate(raw):
        for end, at in enumerate((0, rows - SUB)):
            rows_at = pl.ds(at, SUB)
            view = ref.at[:, :, rows_at, :] if len(ref.shape) == 4 else ref.at[:, rows_at, :]
            copies.append(pltpu.make_async_copy(view, edges[2 * i + end], sems.at[2 * i + end]))
    late = [pltpu.make_async_copy(raw[3 + i], whole[i], sems.at[2 * len(raw) + i]) for i in range(2)]
    for copy in copies + late:
        copy.start()
    for copy in copies:
        copy.wait()
    head, tail = sources(*edges[0::2]), sources(*edges[1::2])
    offs, per = offsets()

    def up(out):
        for f in range(FIELDS):
            for k in range(planes):
                out[pl.ds(per * k + offs[f], BEFORE[f]), :] = src_rows(tail[f], k, pl.ds(SUB - BEFORE[f], BEFORE[f]))

    def down(out):
        for f in range(FIELDS):
            for k in range(planes):
                out[pl.ds(per * k + offs[f], AFTER[f]), :] = src_rows(head[f], k, pl.ds(0, AFTER[f]))

    send(Link("gx", counts["gx"]), outs, up, down)
    for copy in late:
        copy.wait()


def column_lanes(planes):
    firsts, total = [], 0
    for f in range(FIELDS):
        firsts.append(total)
        total += planes * AFTER[f]
    return firsts


def pack_lanes(lane, planes, up):
    out, firsts = jnp.zeros_like(lane), column_lanes(planes)
    for f in range(FIELDS):
        deep = AFTER[f]
        for k in range(planes):
            first = firsts[f] + k * deep
            at = GROUP * (k + 1) + jnp.where(up, 4 - deep, 12)
            out = jnp.where(lane >= first, lane - first + at, out)
    return jnp.minimum(out, LANES - 1)


def unpack_lanes(lane, planes, f):
    deep = AFTER[f]
    step = lax.rem(lane, 4)
    step = jnp.where(lax.rem(lane, GROUP) // 4 == 1, step, step - (4 - deep))
    plane = lane // GROUP - 1
    return jnp.clip(column_lanes(planes)[f] + plane * deep + step, 0, LANES - 1)


def build(counts, dm, ds, ct, w, d, *refs):
    planes, rows = d.shape[0], d.shape[1]
    nx, ny = phases(counts["gx"]), phases(counts["gy"])
    got, (em, es), outs = refs[:nx], refs[nx : nx + 2], refs[nx + 2 :]
    src = sources(dm, ds, ct, w, d)
    offs, per = offsets()
    lane = lane_ids()

    def halo(start, counted, deep):
        def fill(ref):
            for f in range(FIELDS):
                for k in range(planes):
                    if ref is None:
                        at, many = start(deep), deep
                        value = jnp.full((deep, LANES), 1.0 if f == WEIGHT else 0.0, jnp.float32)
                    else:
                        at, many = start(counted[f]), counted[f]
                        value = ref[pl.ds(per * k + offs[f], many), :]
                        value = 1.0 / value if f == WEIGHT else value
                    em[f, k, pl.ds(at, many), :] = value

        return fill

    receive(
        Link("gx", counts["gx"]),
        got,
        halo(lambda n: PAD - n, BEFORE, 3),
        halo(lambda n: PAD + rows, AFTER, 3),
    )
    link = Link("gy", counts["gy"])
    part = lax.rem(lane, GROUP) // 4
    plane_of = lane // GROUP
    own = jnp.logical_or(part == 0, part == 3)
    edges = lax.rem(lane, 4) + jnp.where(part == 0, LANES - 4, 0)
    packing = [pack_lanes(lane, planes, link.even if p == 0 else link.odd) for p in range(ny)]

    def tile(row, read, later):
        for f in range(FIELDS):
            strip = jnp.full((SUB, LANES), 1.0 if f == WEIGHT else 0.0, jnp.float32)
            for k in range(planes):
                strip = jnp.where(jnp.logical_and(own, plane_of == k + 1), take(read(f, k), edges), strip)
            later.put(es, (f, pl.ds(row, SUB), ALL), strip)

    def pack(t, later):
        row = pl.multiple_of(t * SUB, SUB)
        for p in range(ny):
            out = take(es[0, pl.ds(row + SUB, SUB), :], packing[p])
            for f in range(1, FIELDS):
                moved = take(es[f, pl.ds(row + SUB, SUB), :], packing[p])
                out = jnp.where(lane >= column_lanes(planes)[f], moved, out)
            later.put(outs[p], (pl.ds(row, SUB), ALL), out)

    def inner(t, later):
        inside = pl.multiple_of(t * SUB, SUB)
        row = pl.multiple_of(t * SUB + PAD, SUB)

        def read(f, k):
            x = src_rows(src[f], k, pl.ds(inside, SUB))
            x = 1.0 / x if f == WEIGHT else x
            em[f, k, pl.ds(row, SUB), :] = x
            return x

        tile(row, read, later)

    def halos(t, later):
        for row in (PAD - SUB, PAD + rows):
            tile(row, lambda f, k: em[f, k, pl.ds(row, SUB), :], later)

    in_groups(rows // SUB, PAIRED, inner)
    in_groups(1, 1, halos)
    in_groups(sizes(rows)[0], UNROLL, pack)


def fold(strip, group, out, base, tiles):
    group_of = lane_ids() // GROUP
    many = LANES // GROUP
    later = Later()
    for i, some in enumerate(batches(tiles, many)):
        x = None
        for t in some:
            y = turn(strip[pl.ds(SUB * t + SUB, SUB), :], GROUP * (t % many - group))
            x = y if x is None else jnp.where(group_of == t % many, y, x)
        later.put(out, (pl.ds(base + SUB * i, SUB), ALL), x)
    later.flush()


def unfold(read, base, t, group):
    many = LANES // GROUP
    return turn(read(base + SUB * (t // many)), GROUP * (group - t % many))


def sizes(rows):
    tiles = (rows + 2 * PAD - 2 * SUB) // SUB
    folded = SUB * pl.cdiv(tiles * GROUP, LANES)
    return tiles, SUB * tiles, folded


def copy_rows(src, out, base, tiles):
    for some in batches(tiles, 9):
        later = Later()
        for t in some:
            later.put(out, (pl.ds(base + SUB * t, SUB), ALL), src[pl.ds(SUB * t + SUB, SUB), :])
        later.flush()


def plane_out(link, outs, up, down, planes, rows):
    tiles, flat, folded = sizes(rows)

    def put(items, group):
        def write(out):
            for i, (plane, strip) in enumerate(items):
                base = i * (flat + folded)
                copy_rows(plane, out, base, tiles)
                fold(strip, group, out, base + flat, tiles)

        return write

    send(link, outs, put(up, planes), put(down, 1))


def plane_in(link, ins):
    def at(first, known):
        def read(row):
            x = ins[0][pl.ds(row, SUB), :]
            if len(ins) > 1:
                x = jnp.where(first, x, ins[1][pl.ds(row, SUB), :])
            return jnp.where(known, x, 0.0)

        return read

    return at(link.odd, link.before), at(link.even, link.after)


def strips_and_values(counts, em, es, *refs):
    planes, rows = em.shape[1], em.shape[2] - 2 * PAD
    ny = phases(counts["gy"])
    got, (full, v, vs), outs = refs[:ny], refs[ny : ny + 3], refs[ny + 3 :]
    link = Link("gy", counts["gy"])
    row_link = Link("gx", counts["gx"])
    lane = lane_ids()
    part = lax.rem(lane, GROUP) // 4
    near = jnp.logical_or(part == 1, part == 2)
    real_after = jnp.logical_and(part == 1, link.after)
    real_before = jnp.logical_and(part == 2, link.before)
    lanes = [unpack_lanes(lane, planes, f) for f in range(FIELDS)]
    if ny == 1:
        blocks = [(lambda at: got[0][at, :], jnp.logical_or(real_after, real_before))]
    else:
        blocks = [
            (lambda at: jnp.where(link.even, got[0][at, :], got[1][at, :]), real_after),
            (lambda at: jnp.where(link.odd, got[0][at, :], got[1][at, :]), real_before),
        ]
    lost = jnp.logical_and(part == 1, jnp.logical_not(link.after))
    inner = lane // GROUP >= 2
    tiles, flat, folded = sizes(rows)

    def strips(t, later):
        row = pl.multiple_of(SUB * t + SUB, SUB)
        at = pl.ds(pl.multiple_of(SUB * t, SUB), SUB)

        for f in range(FIELDS):
            x = jnp.where(near, 1.0 if f == WEIGHT else 0.0, es[f, pl.ds(row, SUB), :])
            for block, mask in blocks:
                x = jnp.where(mask, take(block(at), lanes[f]), x)
            later.put(full, (f, pl.ds(row, SUB), ALL), x)

    def values(t, later):
        row = pl.multiple_of(SUB * t + SUB, SUB)
        at, lower = pl.ds(row, SUB), pl.ds(row - 1, SUB)
        keep = jnp.logical_or(t < tiles - 1, row_link.after)
        for m in range(2):
            p0, p1, p2 = 3 * m, 3 * m + 1, 3 * m + 2
            s0, s2 = full[p0, at, :], full[p2, at, :]
            x = s0 - jnp.where(inner, turn(s0, GROUP), 0.0)
            x = x + (full[p1, at, :] - full[p1, lower, :])
            x = x + (s2 - turn(s2, 1))
            x = x - INVERSE * full[DATA, at, :]
            later.put(vs, (m, at, ALL), jnp.where(keep, jnp.where(lost, 0.0, x), 0.0))
            last = None
            for k in range(planes):
                x = now = em[p0, k, at, :]
                if k:
                    x = x - last
                last = now
                x = x + (em[p1, k, at, :] - em[p1, k, lower, :])
                y = em[p2, k, at, :]
                x = x + (y - col_before(y, s2, k, lane))
                x = x - INVERSE * em[DATA, k, at, :]
                later.put(v, (m, k, at, ALL), jnp.where(keep, x, 0.0))

    in_groups(tiles, UNROLL, strips)
    in_groups(tiles, UNROLL, values)
    plane_out(
        Link("gz", counts["gz"]),
        outs,
        [(em.at[3 * m, planes - 1], full.at[3 * m]) for m in range(2)],
        [(v.at[m, 0], vs.at[m]) for m in range(2)],
        planes,
        rows,
    )


def settle(first, strip, last, last_strip, below, above, base, has_after, out_first, out_ghost, out_strip, planes, rows):
    tiles, flat, folded = sizes(rows)
    group = lane_ids() // GROUP
    for some in batches(tiles, 6):
        later = Later()
        for t in some:
            at = (pl.ds(SUB * t + SUB, SUB), ALL)
            sent = base + SUB * t
            later.put(out_first, at, first[at] - below(sent))
            later.put(out_ghost, at, jnp.where(has_after, above(sent) - last[at], 0.0))
            x = strip[at]
            x = jnp.where(group == 1, x - unfold(below, base + flat, t, 1), x)
            ghost = unfold(above, base + flat, t, planes + 1) - turn(last_strip[at], GROUP)
            ghost = jnp.where(has_after, ghost, 0.0)
            later.put(out_strip, at, jnp.where(group == planes + 1, ghost, x))
        later.flush()


def pointwise(g, c, p, rw):
    q = g[0] * g[0] + g[1] * g[1] + g[2] * g[2] + SMOOTH
    rn = lax.rsqrt(q)
    tn = STEP * (q * rn)
    rden = 1.0 / (1.0 + tn * rw)
    inner = c[0] * p[0] + c[1] * p[1] + c[2] * p[2]
    inner = inner + STEP * (c[0] * g[0] + c[1] * g[1] + c[2] * g[2])
    s = inner * rden * (rden * rw)
    wpart = s * (tn * rw)
    scale = STEP * rden
    along = (-STEP) * s * rn
    return [scale * c[a] + along * g[a] for a in range(3)], rden, wpart


class Around:
    def __init__(self, plane, strip, planes, row, lane):
        self.plane, self.planes, self.lane = plane, planes, lane
        self.at, self.upper = pl.ds(row, SUB), pl.ds(row + 1, SUB)
        self.strip = strip
        self.s = strip[self.at, :]
        self.now = [plane(k)[self.at, :] for k in range(planes + 1)]

    def steps(self, k):
        x = self.now[k]
        return (
            self.now[k + 1] - x,
            self.plane(k)[self.upper, :] - x,
            col_after(x, self.s, k, self.lane) - x,
        )

    def strip_steps(self):
        x = self.s
        return turn(x, -GROUP) - x, self.strip[self.upper, :] - x, turn(x, -1) - x


class Back:
    def __init__(self, carried, lane):
        self.carried, self.lane = carried, lane
        self.top = lax.broadcasted_iota(jnp.int32, (SUB, LANES), 0) == 0
        self.last, self.out = None, []

    def row_before(self, x):
        down = pltpu.roll(x, 1, 0)
        before = jnp.where(self.top, self.carried[len(self.out)], down)
        self.out.append(down)
        return before

    def strip(self, cg):
        self.s = cg[2]
        x = cg[0] - jnp.where(self.lane // GROUP >= 2, turn(cg[0], GROUP), 0.0)
        x = x + (cg[1] - self.row_before(cg[1]))
        return x + (cg[2] - turn(cg[2], 1))

    def plane(self, k, cg):
        x = cg[0] if self.last is None else cg[0] - self.last
        self.last = cg[0]
        x = x + (cg[1] - self.row_before(cg[1]))
        return x + (cg[2] - col_before(cg[2], self.s, k, self.lane))


def over_tiles(tiles, planes, step):
    together = TOGETHER
    while tiles % together:
        together -= 1

    def body(t, carried):
        later = Later()
        for u in range(together):
            carried = step(t * together + u, carried, later)
        later.flush()
        return tuple(carried)

    lax.fori_loop(0, tiles // together, body, (jnp.zeros((SUB, LANES), jnp.float32),) * (planes + 1))


def chooser(mid, first, ghost, planes):
    return lambda k: first if k == 0 else ghost if k == planes else mid.at[k]


def first_step(counts, em, full, v, vs, *refs):
    planes, rows = em.shape[1], em.shape[2] - 2 * PAD
    nz = phases(counts["gz"])
    got, refs = refs[:nz], refs[nz:]
    (r, rs, rd, rds, wp, top, tops), outs, scratch = refs[:7], refs[7 : 7 + nz], refs[7 + nz :]
    first, ghost, strip = scratch
    link, row_link, col_link = (Link(a, counts[a]) for a in ("gz", "gx", "gy"))
    lane = lane_ids()
    lost = jnp.logical_and(lax.rem(lane, GROUP) // 4 == 1, jnp.logical_not(col_link.after))
    tiles, flat, folded = sizes(rows)
    below, above = plane_in(link, got)
    settle(v.at[0, 0], vs.at[0], em.at[0, planes - 1], full.at[0], below, above, 0, link.after, first, ghost, strip, planes, rows)

    def step(t, carried, later):
        row = pl.multiple_of(SUB * t + SUB, SUB)
        at = pl.ds(row, SUB)
        keep = jnp.logical_or(t < tiles - 1, row_link.after)
        field = Around(chooser(v.at[0], first, ghost, planes), strip, planes, row, lane)
        back = Back(carried, lane)
        cg, rden, _ = pointwise(
            field.strip_steps(), [full[6 + a, at, :] for a in range(3)], [full[a, at, :] for a in range(3)], full[WEIGHT, at, :]
        )
        later.put(rds, (at, ALL), rden)
        later.put(tops, (at, ALL), cg[0])
        later.put(rs, (at, ALL), jnp.where(keep, jnp.where(lost, 0.0, back.strip(cg)), 0.0))
        for k in range(planes):
            cg, rden, wpart = pointwise(
                field.steps(k), [em[6 + a, k, at, :] for a in range(3)], [em[a, k, at, :] for a in range(3)], em[WEIGHT, k, at, :]
            )
            later.put(rd, (k, at, ALL), rden)
            later.put(wp, (k, at, ALL), wpart)
            later.put(r, (k, at, ALL), jnp.where(keep, back.plane(k, cg), 0.0))
            if k == planes - 1:
                later.put(top, (at, ALL), cg[0])
        return back.out

    over_tiles(tiles, planes, step)
    plane_out(link, outs, [(top, tops)], [(r.at[0], rs)], planes, rows)


def second_step(counts, em, full, v, vs, *refs):
    planes, rows = em.shape[1], em.shape[2] - 2 * PAD
    nz = phases(counts["gz"])
    got_v, refs = refs[:nz], refs[nz:]
    (r1, r1s, rd, rds, wp, top1, top1s), refs = refs[:7], refs[7:]
    got_r, refs = refs[:nz], refs[nz:]
    (x, r2, r2s, top, tops, wg, dg), outs, scratch = refs[:7], refs[7 : 7 + nz], refs[7 + nz :]
    first, ghost, strip, first_r, ghost_r, strip_r = scratch
    link, row_link, col_link = (Link(a, counts[a]) for a in ("gz", "gx", "gy"))
    lane = lane_ids()
    part = lax.rem(lane, GROUP) // 4
    lost = jnp.logical_and(part == 1, jnp.logical_not(col_link.after))
    outside = jnp.logical_and(part == 2, jnp.logical_not(col_link.before))
    tiles, flat, folded = sizes(rows)
    below, above = plane_in(link, got_v)
    settle(
        v.at[1, 0], vs.at[1], em.at[3, planes - 1], full.at[3], below, above, flat + folded, link.after, first, ghost, strip, planes, rows
    )
    below_r, above_r = plane_in(link, got_r)
    settle(r1.at[0], r1s, top1, top1s, below_r, above_r, 0, link.after, first_r, ghost_r, strip_r, planes, rows)

    def step(t, carried, later):
        row = pl.multiple_of(SUB * t + SUB, SUB)
        at = pl.ds(row, SUB)
        keep = jnp.logical_or(t < tiles - 1, row_link.after)
        inside = jnp.logical_or(t > 0, row_link.before)
        field = Around(chooser(v.at[1], first, ghost, planes), strip, planes, row, lane)
        spread = Around(chooser(r1, first_r, ghost_r, planes), strip_r, planes, row, lane)
        back = Back(carried, lane)
        rden = rds[at, :]
        down = spread.strip_steps()
        c = [jnp.where(inside, jnp.where(outside, 0.0, full[6 + a, at, :] * rden + down[a]), 0.0) for a in range(3)]
        cg, _, _ = pointwise(field.strip_steps(), c, [full[3 + a, at, :] for a in range(3)], full[WEIGHT, at, :])
        later.put(tops, (at, ALL), cg[0])
        later.put(r2s, (at, ALL), jnp.where(keep, jnp.where(lost, 0.0, back.strip(cg)), 0.0))
        for k in range(planes):
            rden = rd[k, at, :]
            down = spread.steps(k)
            c = [jnp.where(inside, em[6 + a, k, at, :] * rden + down[a], 0.0) for a in range(3)]
            cg, rden, wpart = pointwise(field.steps(k), c, [em[3 + a, k, at, :] for a in range(3)], em[WEIGHT, k, at, :])
            for a in range(3):
                later.put(x, (a, k, at, ALL), c[a] * rden)
            later.put(wg, (k, at, ALL), wp[k, at, :] + wpart)
            later.put(dg, (k, at, ALL), spread.now[k])
            later.put(r2, (k, at, ALL), jnp.where(keep, back.plane(k, cg), 0.0))
            if k == planes - 1:
                later.put(top, (at, ALL), cg[0])
        return back.out

    over_tiles(tiles, planes, step)
    plane_out(link, outs, [(top, tops)], [(r2.at[0], r2s)], planes, rows)


def finish(counts, x, r2, r2s, top, tops, wg, dg, *refs):
    planes, rows = r2.shape[0], r2.shape[1] - 2 * PAD
    nz = phases(counts["gz"])
    got, (grad, weight_grad, data_grad), scratch = refs[:nz], refs[nz : nz + 3], refs[nz + 3 :]
    first, ghost, strip = scratch
    link = Link("gz", counts["gz"])
    lane = lane_ids()
    below, above = plane_in(link, got)
    settle(r2.at[0], r2s, top, tops, below, above, 0, link.after, first, ghost, strip, planes, rows)

    def step(t, later):
        row = pl.multiple_of(SUB * t + PAD, SUB)
        at, to = pl.ds(row, SUB), pl.ds(pl.multiple_of(SUB * t, SUB), SUB)
        spread = Around(chooser(r2, first, ghost, planes), strip, planes, row, lane)
        for k in range(planes):
            down = spread.steps(k)
            for a in range(3):
                later.put(grad, (a, k, to, ALL), x[a, k, at, :] + down[a])
            later.put(weight_grad, (k, to, ALL), wg[k, at, :])
            later.put(data_grad, (k, to, ALL), INVERSE * (dg[k, at, :] + spread.now[k]))

    in_groups(rows // SUB, LAST, step)


def call(body, counts, operands, outs, scratch=(), space=pltpu.VMEM, grant=16):
    held = pl.BlockSpec(memory_space=pltpu.VMEM)
    return pl.pallas_call(
        functools.partial(body, counts),
        out_shape=outs,
        in_specs=[pl.BlockSpec(memory_space=space)] * len(operands),
        out_specs=[held] * len(outs),
        scratch_shapes=list(scratch),
        compiler_params=pltpu.CompilerParams(vmem_limit_bytes=grant * 1024 * 1024),
        name=body.__name__,
    )(*operands)


def vmem(*shape):
    return pltpu.VMEM(shape, jnp.float32)


def shards(counts, data, weight, dual_start, dual_mid, cotangent):
    planes, rows, cols = data.shape
    held = rows + 2 * PAD
    tiles, flat, folded = sizes(rows)
    nx, ny, nz = (phases(counts[a]) for a in ("gx", "gy", "gz"))
    raw = (dual_mid, dual_start, cotangent, weight, data)
    block, strip, line = vmem(planes, held, cols), vmem(held, LANES), vmem(held, cols)

    near_weight, near_data, *sent = call(
        rows_out,
        counts,
        raw,
        [vmem(*data.shape)] * 2 + [vmem(planes * offsets()[1], cols)] * nx,
        [vmem(*x.shape[:-2], SUB, cols) for x in raw for _ in range(2)] + [pltpu.SemaphoreType.DMA((2 * len(raw) + 2,))],
        pltpu.HBM,
        60,
    )
    got = swap(sent, "gx", counts)
    em, es, *sent = call(
        build, counts, (*raw[:3], near_weight, near_data, *got), [vmem(FIELDS, planes, held, cols), vmem(FIELDS, held, LANES)] + [vmem(flat, LANES)] * ny
    )
    got = swap(sent, "gy", counts)
    one = flat + folded
    full, v, vs, *sent = call(
        strips_and_values,
        counts,
        (em, es, *got),
        [vmem(FIELDS, held, LANES), vmem(2, planes, held, cols), vmem(2, held, LANES)] + [vmem(2 * one, LANES)] * nz,
    )
    got_v = swap(sent, "gz", counts)
    state = [block, strip, block, strip, block, line, strip]
    work = [line, line, strip]
    *first, = call(
        first_step,
        counts,
        (em, full, v, vs, *got_v),
        state + [vmem(one, LANES)] * nz,
        work,
    )
    got_r = swap(first[7:], "gz", counts)
    *second, = call(
        second_step,
        counts,
        (em, full, v, vs, *got_v, *first[:7], *got_r),
        [vmem(3, planes, held, cols), block, strip, line, strip, block, block] + [vmem(one, LANES)] * nz,
        work + work,
    )
    got = swap(second[7:], "gz", counts)
    out = jax.ShapeDtypeStruct
    return tuple(call(
        finish,
        counts,
        (*second[:7], *got),
        [out(dual_mid.shape, jnp.float32), out(data.shape, jnp.float32), out(data.shape, jnp.float32)],
        work,
    ))


def solution(mesh):
    field, dual = P("gz", "gx", "gy"), P(None, "gz", "gx", "gy")
    return jax.shard_map(
        functools.partial(shards, dict(mesh.shape)),
        mesh=mesh,
        in_specs=(field, field, dual, dual, dual),
        out_specs=(dual, field, field),
        check_vma=False,
    )
```

```python
import functools

import jax
import jax.numpy as jnp
from jax import lax
from jax.experimental import pallas as pl
from jax.experimental.pallas import tpu as pltpu
from jax.sharding import PartitionSpec as P


STEP = 0.08
INVERSE = 0.5
SMOOTH = 0.01

AFTER = (3, 3, 3, 2, 2, 2, 2, 2, 2, 2, 3)
BEFORE = (2, 3, 2, 1, 2, 1, 2, 2, 2, 2, 2)
FIELDS = len(AFTER)
WEIGHT, DATA = 9, 10
PAD = 16
SUB = 8
UNROLL = 18
TOGETHER = 6
PAIRED = 4
LAST = 16
LANES = 128
GROUP = 16


class Link:
    def __init__(self, axis, count):
        place = lax.axis_index(axis)
        self.even = lax.rem(place, 2) == 0
        self.odd = jnp.logical_not(self.even)
        self.before = place > 0
        self.after = place < count - 1


def phases(count):
    return 1 if count == 2 else 2


def swap(values, axis, counts):
    spare = "gx" if axis == "gy" else "gy"
    names = tuple(n for n in counts if n in (axis, spare))
    count, wide = counts[axis], counts[spare]

    def place(i, j):
        return i * wide + j if names[0] == axis else j * count + i

    pairs = [[(place(i, j), place(i + 1, j)) for i in range(0, count, 2) for j in range(wide)]]
    if count > 2:
        pairs.append([(place(i, j), place(i + 1, j)) for i in range(1, count - 1, 2) for j in range(wide)])
        pairs[1] += [(place(i, j), place(i, j + 1)) for i in (0, count - 1) for j in range(0, wide, 2)]
    return [lax.ppermute(x, names, [q for a, b in some for q in ((a, b), (b, a))]) for x, some in zip(values, pairs)]


def send(link, outs, up, down):
    @pl.when(link.even)
    def _():
        up(outs[0])
        if len(outs) > 1:
            down(outs[1])

    @pl.when(link.odd)
    def _():
        down(outs[0])
        if len(outs) > 1:
            up(outs[1])


def receive(link, ins, before, after):
    pl.when(link.odd)(lambda: before(ins[0]))
    pl.when(link.even)(lambda: after(ins[0]))
    if len(ins) > 1:
        pl.when(jnp.logical_and(link.even, link.before))(lambda: before(ins[1]))
        pl.when(jnp.logical_and(link.odd, link.after))(lambda: after(ins[1]))
    pl.when(jnp.logical_not(link.before))(lambda: before(None))
    pl.when(jnp.logical_not(link.after))(lambda: after(None))


class Later:
    def __init__(self):
        self.items = []

    def put(self, ref, index, value):
        self.items.append((ref, index, value))

    def flush(self):
        for ref, index, value in self.items:
            ref[index] = value


ALL = slice(None)


def in_groups(count, together, step):
    while count % together:
        together -= 1

    def body(t):
        later = Later()
        for u in range(together):
            step(t * together + u, later)
        later.flush()

    if together == count:
        body(0)
    else:
        pl.loop(0, count // together)(body)


def batches(count, size):
    return [range(i, min(i + size, count)) for i in range(0, count, size)]


def lane_ids():
    return lax.broadcasted_iota(jnp.int32, (SUB, LANES), 1)


def turn(x, by):
    return pltpu.roll(x, by % LANES if isinstance(by, int) else lax.rem(by + 4 * LANES, LANES), 1)


def take(x, lanes):
    return jnp.take_along_axis(x, lanes, axis=1)


def col_before(x, strip, k, lane):
    return jnp.where(lane == 0, turn(strip, -(GROUP * (k + 1) + 11)), turn(x, 1))


def col_after(x, strip, k, lane):
    return jnp.where(lane == LANES - 1, turn(strip, LANES - 1 - (GROUP * (k + 1) + 4)), turn(x, -1))


def sources(dm, ds, ct, w, d):
    return [(r, a) for r in (dm, ds, ct) for a in range(3)] + [(w, None), (d, None)]


def src_rows(source, k, rows):
    ref, a = source
    return ref[k, rows, :] if a is None else ref[a, k, rows, :]


def offsets():
    out, total = [], 0
    for f in range(FIELDS):
        out.append(total)
        total += AFTER[f]
    return out, total


def rows_out(counts, *refs):
    nx = phases(counts["gx"])
    raw, outs, (*edges, sems) = refs[:5], refs[5 : 5 + nx], refs[5 + nx :]
    planes, rows = raw[4].shape[0], raw[4].shape[1]
    copies = []
    for i, ref in enumerate(raw):
        for end, at in enumerate((0, rows - SUB)):
            rows_at = pl.ds(at, SUB)
            view = ref.at[:, :, rows_at, :] if len(ref.shape) == 4 else ref.at[:, rows_at, :]
            copies.append(pltpu.make_async_copy(view, edges[2 * i + end], sems.at[2 * i + end]))
    for copy in copies:
        copy.start()
    for copy in copies:
        copy.wait()
    head, tail = sources(*edges[0::2]), sources(*edges[1::2])
    offs, per = offsets()

    def up(out):
        for f in range(FIELDS):
            for k in range(planes):
                out[pl.ds(per * k + offs[f], BEFORE[f]), :] = src_rows(tail[f], k, pl.ds(SUB - BEFORE[f], BEFORE[f]))

    def down(out):
        for f in range(FIELDS):
            for k in range(planes):
                out[pl.ds(per * k + offs[f], AFTER[f]), :] = src_rows(head[f], k, pl.ds(0, AFTER[f]))

    send(Link("gx", counts["gx"]), outs, up, down)

def column_lanes(planes):
    firsts, total = [], 0
    for f in range(FIELDS):
        firsts.append(total)
        total += planes * AFTER[f]
    return firsts


def pack_lanes(lane, planes, up):
    out, firsts = jnp.zeros_like(lane), column_lanes(planes)
    for f in range(FIELDS):
        deep = AFTER[f]
        for k in range(planes):
            first = firsts[f] + k * deep
            at = GROUP * (k + 1) + jnp.where(up, 4 - deep, 12)
            out = jnp.where(lane >= first, lane - first + at, out)
    return jnp.minimum(out, LANES - 1)


def unpack_lanes(lane, planes, f):
    deep = AFTER[f]
    step = lax.rem(lane, 4)
    step = jnp.where(lax.rem(lane, GROUP) // 4 == 1, step, step - (4 - deep))
    plane = lane // GROUP - 1
    return jnp.clip(column_lanes(planes)[f] + plane * deep + step, 0, LANES - 1)


class Strips:
    def __init__(self, counts, planes, em, es, outs):
        self.planes, self.em, self.es, self.outs = planes, em, es, outs
        link = Link("gy", counts["gy"])
        self.lane = lane = lane_ids()
        part = lax.rem(lane, GROUP) // 4
        own = jnp.logical_or(part == 0, part == 3)
        self.mine = [jnp.logical_and(own, lane // GROUP == k + 1) for k in range(planes)]
        self.edges = lax.rem(lane, 4) + jnp.where(part == 0, LANES - 4, 0)
        self.packing = [pack_lanes(lane, planes, link.even if p == 0 else link.odd) for p in range(len(outs))]

    def build(self, row, later, invert):
        at = pl.ds(row, SUB)
        for f in range(FIELDS):
            strip = jnp.full((SUB, LANES), 1.0 if f == WEIGHT else 0.0, jnp.float32)
            for k in range(self.planes):
                x = self.em[f, k, at, :]
                if invert and f == WEIGHT:
                    x = 1.0 / x
                    later.put(self.em, (f, k, at, ALL), x)
                strip = jnp.where(self.mine[k], take(x, self.edges), strip)
            later.put(self.es, (f, at, ALL), strip)

    def pack(self, row, later):
        firsts = column_lanes(self.planes)
        for p, out in enumerate(self.outs):
            packed = take(self.es[0, pl.ds(row, SUB), :], self.packing[p])
            for f in range(1, FIELDS):
                moved = take(self.es[f, pl.ds(row, SUB), :], self.packing[p])
                packed = jnp.where(self.lane >= firsts[f], moved, packed)
            later.put(out, (pl.ds(row - SUB, SUB), ALL), packed)


def inside(counts, dm, ds, ct, w, d, em, es, *refs):
    planes, rows = d.shape[0], d.shape[1]
    outs, sems = refs[:-1], refs[-1]
    copies, f = [], 0
    for i, ref in enumerate((dm, ds, ct, w, d)):
        if len(ref.shape) == 4:
            to = em.at[pl.ds(f, ref.shape[0]), :, pl.ds(PAD, rows), :]
            f += ref.shape[0]
        else:
            to = em.at[f, :, pl.ds(PAD, rows), :]
            f += 1
        copies.append(pltpu.make_async_copy(ref, to, sems.at[i]))
    for copy in copies:
        copy.start()
    for copy in copies:
        copy.wait()
    strips = Strips(counts, planes, em, es, outs)
    in_groups(rows // SUB, PAIRED, lambda t, later: strips.build(pl.multiple_of(t * SUB + PAD, SUB), later, True))
    in_groups(rows // SUB, UNROLL, lambda t, later: strips.pack(pl.multiple_of(t * SUB + PAD, SUB), later))


def outside(counts, *refs):
    nx, ny = phases(counts["gx"]), phases(counts["gy"])
    got, (em, es, *outs) = refs[2 + ny : 2 + ny + nx], refs[2 + ny + nx :]
    planes, rows = em.shape[1], em.shape[2] - 2 * PAD
    offs, per = offsets()

    def halo(start, counted, deep):
        def fill(ref):
            for f in range(FIELDS):
                for k in range(planes):
                    if ref is None:
                        at, many = start(deep), deep
                        value = jnp.full((deep, LANES), 1.0 if f == WEIGHT else 0.0, jnp.float32)
                    else:
                        at, many = start(counted[f]), counted[f]
                        value = ref[pl.ds(per * k + offs[f], many), :]
                        value = 1.0 / value if f == WEIGHT else value
                    em[f, k, pl.ds(at, many), :] = value

        return fill

    receive(
        Link("gx", counts["gx"]),
        got,
        halo(lambda n: PAD - n, BEFORE, 3),
        halo(lambda n: PAD + rows, AFTER, 3),
    )
    strips = Strips(counts, planes, em, es, outs)
    later = Later()
    for row in (PAD - SUB, PAD + rows):
        strips.build(row, later, False)
    later.flush()
    later = Later()
    for row in (PAD - SUB, PAD + rows):
        strips.pack(row, later)
    later.flush()


def fold(strip, group, out, base, tiles):
    group_of = lane_ids() // GROUP
    many = LANES // GROUP
    later = Later()
    for i, some in enumerate(batches(tiles, many)):
        x = None
        for t in some:
            y = turn(strip[pl.ds(SUB * t + SUB, SUB), :], GROUP * (t % many - group))
            x = y if x is None else jnp.where(group_of == t % many, y, x)
        later.put(out, (pl.ds(base + SUB * i, SUB), ALL), x)
    later.flush()


def unfold(read, base, t, group):
    many = LANES // GROUP
    return turn(read(base + SUB * (t // many)), GROUP * (group - t % many))


def sizes(rows):
    tiles = (rows + 2 * PAD - 2 * SUB) // SUB
    folded = SUB * pl.cdiv(tiles * GROUP, LANES)
    return tiles, SUB * tiles, folded


def copy_rows(src, out, base, tiles):
    for some in batches(tiles, 9):
        later = Later()
        for t in some:
            later.put(out, (pl.ds(base + SUB * t, SUB), ALL), src[pl.ds(SUB * t + SUB, SUB), :])
        later.flush()


def plane_out(link, outs, up, down, planes, rows):
    tiles, flat, folded = sizes(rows)

    def put(items, group):
        def write(out):
            for i, (plane, strip) in enumerate(items):
                base = i * (flat + folded)
                copy_rows(plane, out, base, tiles)
                fold(strip, group, out, base + flat, tiles)

        return write

    send(link, outs, put(up, planes), put(down, 1))


def plane_in(link, ins):
    def at(first, known):
        def read(row):
            x = ins[0][pl.ds(row, SUB), :]
            if len(ins) > 1:
                x = jnp.where(first, x, ins[1][pl.ds(row, SUB), :])
            return jnp.where(known, x, 0.0)

        return read

    return at(link.odd, link.before), at(link.even, link.after)


def strips_and_values(counts, em, es, *refs):
    planes, rows = em.shape[1], em.shape[2] - 2 * PAD
    ny = phases(counts["gy"])
    got, (full, v, vs), outs = refs[:ny], refs[ny : ny + 3], refs[ny + 3 :]
    link = Link("gy", counts["gy"])
    row_link = Link("gx", counts["gx"])
    lane = lane_ids()
    part = lax.rem(lane, GROUP) // 4
    near = jnp.logical_or(part == 1, part == 2)
    real_after = jnp.logical_and(part == 1, link.after)
    real_before = jnp.logical_and(part == 2, link.before)
    lanes = [unpack_lanes(lane, planes, f) for f in range(FIELDS)]
    if ny == 1:
        blocks = [(lambda at: got[0][at, :], jnp.logical_or(real_after, real_before))]
    else:
        blocks = [
            (lambda at: jnp.where(link.even, got[0][at, :], got[1][at, :]), real_after),
            (lambda at: jnp.where(link.odd, got[0][at, :], got[1][at, :]), real_before),
        ]
    lost = jnp.logical_and(part == 1, jnp.logical_not(link.after))
    inner = lane // GROUP >= 2
    tiles, flat, folded = sizes(rows)

    def strips(t, later):
        row = pl.multiple_of(SUB * t + SUB, SUB)
        at = pl.ds(pl.multiple_of(SUB * t, SUB), SUB)

        for f in range(FIELDS):
            x = jnp.where(near, 1.0 if f == WEIGHT else 0.0, es[f, pl.ds(row, SUB), :])
            for block, mask in blocks:
                x = jnp.where(mask, take(block(at), lanes[f]), x)
            later.put(full, (f, pl.ds(row, SUB), ALL), x)

    def values(t, later):
        row = pl.multiple_of(SUB * t + SUB, SUB)
        at, lower = pl.ds(row, SUB), pl.ds(row - 1, SUB)
        keep = jnp.logical_or(t < tiles - 1, row_link.after)
        for m in range(2):
            p0, p1, p2 = 3 * m, 3 * m + 1, 3 * m + 2
            s0, s2 = full[p0, at, :], full[p2, at, :]
            x = s0 - jnp.where(inner, turn(s0, GROUP), 0.0)
            x = x + (full[p1, at, :] - full[p1, lower, :])
            x = x + (s2 - turn(s2, 1))
            x = x - INVERSE * full[DATA, at, :]
            later.put(vs, (m, at, ALL), jnp.where(keep, jnp.where(lost, 0.0, x), 0.0))
            last = None
            for k in range(planes):
                x = now = em[p0, k, at, :]
                if k:
                    x = x - last
                last = now
                x = x + (em[p1, k, at, :] - em[p1, k, lower, :])
                y = em[p2, k, at, :]
                x = x + (y - col_before(y, s2, k, lane))
                x = x - INVERSE * em[DATA, k, at, :]
                later.put(v, (m, k, at, ALL), jnp.where(keep, x, 0.0))

    in_groups(tiles, UNROLL, strips)
    in_groups(tiles, UNROLL, values)
    plane_out(
        Link("gz", counts["gz"]),
        outs,
        [(em.at[3 * m, planes - 1], full.at[3 * m]) for m in range(2)],
        [(v.at[m, 0], vs.at[m]) for m in range(2)],
        planes,
        rows,
    )


def settle(first, strip, last, last_strip, below, above, base, has_after, out_first, out_ghost, out_strip, planes, rows):
    tiles, flat, folded = sizes(rows)
    group = lane_ids() // GROUP
    for some in batches(tiles, 6):
        later = Later()
        for t in some:
            at = (pl.ds(SUB * t + SUB, SUB), ALL)
            sent = base + SUB * t
            later.put(out_first, at, first[at] - below(sent))
            later.put(out_ghost, at, jnp.where(has_after, above(sent) - last[at], 0.0))
            x = strip[at]
            x = jnp.where(group == 1, x - unfold(below, base + flat, t, 1), x)
            ghost = unfold(above, base + flat, t, planes + 1) - turn(last_strip[at], GROUP)
            ghost = jnp.where(has_after, ghost, 0.0)
            later.put(out_strip, at, jnp.where(group == planes + 1, ghost, x))
        later.flush()


def pointwise(g, c, p, rw):
    q = g[0] * g[0] + g[1] * g[1] + g[2] * g[2] + SMOOTH
    rn = lax.rsqrt(q)
    tn = STEP * (q * rn)
    rden = 1.0 / (1.0 + tn * rw)
    inner = c[0] * p[0] + c[1] * p[1] + c[2] * p[2]
    inner = inner + STEP * (c[0] * g[0] + c[1] * g[1] + c[2] * g[2])
    s = inner * rden * (rden * rw)
    wpart = s * (tn * rw)
    scale = STEP * rden
    along = (-STEP) * s * rn
    return [scale * c[a] + along * g[a] for a in range(3)], rden, wpart


class Around:
    def __init__(self, plane, strip, planes, row, lane):
        self.plane, self.planes, self.lane = plane, planes, lane
        self.at, self.upper = pl.ds(row, SUB), pl.ds(row + 1, SUB)
        self.strip = strip
        self.s = strip[self.at, :]
        self.now = [plane(k)[self.at, :] for k in range(planes + 1)]

    def steps(self, k):
        x = self.now[k]
        return (
            self.now[k + 1] - x,
            self.plane(k)[self.upper, :] - x,
            col_after(x, self.s, k, self.lane) - x,
        )

    def strip_steps(self):
        x = self.s
        return turn(x, -GROUP) - x, self.strip[self.upper, :] - x, turn(x, -1) - x


class Back:
    def __init__(self, carried, lane):
        self.carried, self.lane = carried, lane
        self.top = lax.broadcasted_iota(jnp.int32, (SUB, LANES), 0) == 0
        self.last, self.out = None, []

    def row_before(self, x):
        down = pltpu.roll(x, 1, 0)
        before = jnp.where(self.top, self.carried[len(self.out)], down)
        self.out.append(down)
        return before

    def strip(self, cg):
        self.s = cg[2]
        x = cg[0] - jnp.where(self.lane // GROUP >= 2, turn(cg[0], GROUP), 0.0)
        x = x + (cg[1] - self.row_before(cg[1]))
        return x + (cg[2] - turn(cg[2], 1))

    def plane(self, k, cg):
        x = cg[0] if self.last is None else cg[0] - self.last
        self.last = cg[0]
        x = x + (cg[1] - self.row_before(cg[1]))
        return x + (cg[2] - col_before(cg[2], self.s, k, self.lane))


def over_tiles(tiles, planes, step):
    together = TOGETHER
    while tiles % together:
        together -= 1

    def body(t, carried):
        later = Later()
        for u in range(together):
            carried = step(t * together + u, carried, later)
        later.flush()
        return tuple(carried)

    lax.fori_loop(0, tiles // together, body, (jnp.zeros((SUB, LANES), jnp.float32),) * (planes + 1))


def chooser(mid, first, ghost, planes):
    return lambda k: first if k == 0 else ghost if k == planes else mid.at[k]


def first_step(counts, em, full, v, vs, *refs):
    planes, rows = em.shape[1], em.shape[2] - 2 * PAD
    nz = phases(counts["gz"])
    got, refs = refs[:nz], refs[nz:]
    (r, rs, rd, rds, wp, top, tops), outs, scratch = refs[:7], refs[7 : 7 + nz], refs[7 + nz :]
    first, ghost, strip = scratch
    link, row_link, col_link = (Link(a, counts[a]) for a in ("gz", "gx", "gy"))
    lane = lane_ids()
    lost = jnp.logical_and(lax.rem(lane, GROUP) // 4 == 1, jnp.logical_not(col_link.after))
    tiles, flat, folded = sizes(rows)
    below, above = plane_in(link, got)
    settle(v.at[0, 0], vs.at[0], em.at[0, planes - 1], full.at[0], below, above, 0, link.after, first, ghost, strip, planes, rows)

    def step(t, carried, later):
        row = pl.multiple_of(SUB * t + SUB, SUB)
        at = pl.ds(row, SUB)
        keep = jnp.logical_or(t < tiles - 1, row_link.after)
        field = Around(chooser(v.at[0], first, ghost, planes), strip, planes, row, lane)
        back = Back(carried, lane)
        cg, rden, _ = pointwise(
            field.strip_steps(), [full[6 + a, at, :] for a in range(3)], [full[a, at, :] for a in range(3)], full[WEIGHT, at, :]
        )
        later.put(rds, (at, ALL), rden)
        later.put(tops, (at, ALL), cg[0])
        later.put(rs, (at, ALL), jnp.where(keep, jnp.where(lost, 0.0, back.strip(cg)), 0.0))
        for k in range(planes):
            cg, rden, wpart = pointwise(
                field.steps(k), [em[6 + a, k, at, :] for a in range(3)], [em[a, k, at, :] for a in range(3)], em[WEIGHT, k, at, :]
            )
            later.put(rd, (k, at, ALL), rden)
            later.put(wp, (k, at, ALL), wpart)
            later.put(r, (k, at, ALL), jnp.where(keep, back.plane(k, cg), 0.0))
            if k == planes - 1:
                later.put(top, (at, ALL), cg[0])
        return back.out

    over_tiles(tiles, planes, step)
    plane_out(link, outs, [(top, tops)], [(r.at[0], rs)], planes, rows)


def second_step(counts, em, full, v, vs, *refs):
    planes, rows = em.shape[1], em.shape[2] - 2 * PAD
    nz = phases(counts["gz"])
    got_v, refs = refs[:nz], refs[nz:]
    (r1, r1s, rd, rds, wp, top1, top1s), refs = refs[:7], refs[7:]
    got_r, refs = refs[:nz], refs[nz:]
    (x, r2, r2s, top, tops, wg, dg), outs, scratch = refs[:7], refs[7 : 7 + nz], refs[7 + nz :]
    first, ghost, strip, first_r, ghost_r, strip_r = scratch
    link, row_link, col_link = (Link(a, counts[a]) for a in ("gz", "gx", "gy"))
    lane = lane_ids()
    part = lax.rem(lane, GROUP) // 4
    lost = jnp.logical_and(part == 1, jnp.logical_not(col_link.after))
    outside = jnp.logical_and(part == 2, jnp.logical_not(col_link.before))
    tiles, flat, folded = sizes(rows)
    below, above = plane_in(link, got_v)
    settle(
        v.at[1, 0], vs.at[1], em.at[3, planes - 1], full.at[3], below, above, flat + folded, link.after, first, ghost, strip, planes, rows
    )
    below_r, above_r = plane_in(link, got_r)
    settle(r1.at[0], r1s, top1, top1s, below_r, above_r, 0, link.after, first_r, ghost_r, strip_r, planes, rows)

    def step(t, carried, later):
        row = pl.multiple_of(SUB * t + SUB, SUB)
        at = pl.ds(row, SUB)
        keep = jnp.logical_or(t < tiles - 1, row_link.after)
        inside = jnp.logical_or(t > 0, row_link.before)
        field = Around(chooser(v.at[1], first, ghost, planes), strip, planes, row, lane)
        spread = Around(chooser(r1, first_r, ghost_r, planes), strip_r, planes, row, lane)
        back = Back(carried, lane)
        rden = rds[at, :]
        down = spread.strip_steps()
        c = [jnp.where(inside, jnp.where(outside, 0.0, full[6 + a, at, :] * rden + down[a]), 0.0) for a in range(3)]
        cg, _, _ = pointwise(field.strip_steps(), c, [full[3 + a, at, :] for a in range(3)], full[WEIGHT, at, :])
        later.put(tops, (at, ALL), cg[0])
        later.put(r2s, (at, ALL), jnp.where(keep, jnp.where(lost, 0.0, back.strip(cg)), 0.0))
        for k in range(planes):
            rden = rd[k, at, :]
            down = spread.steps(k)
            c = [jnp.where(inside, em[6 + a, k, at, :] * rden + down[a], 0.0) for a in range(3)]
            cg, rden, wpart = pointwise(field.steps(k), c, [em[3 + a, k, at, :] for a in range(3)], em[WEIGHT, k, at, :])
            for a in range(3):
                later.put(x, (a, k, at, ALL), c[a] * rden)
            later.put(wg, (k, at, ALL), wp[k, at, :] + wpart)
            later.put(dg, (k, at, ALL), spread.now[k])
            later.put(r2, (k, at, ALL), jnp.where(keep, back.plane(k, cg), 0.0))
            if k == planes - 1:
                later.put(top, (at, ALL), cg[0])
        return back.out

    over_tiles(tiles, planes, step)
    plane_out(link, outs, [(top, tops)], [(r2.at[0], r2s)], planes, rows)


def finish(counts, x, r2, r2s, top, tops, wg, dg, *refs):
    planes, rows = r2.shape[0], r2.shape[1] - 2 * PAD
    nz = phases(counts["gz"])
    got, (grad, weight_grad, data_grad), scratch = refs[:nz], refs[nz : nz + 3], refs[nz + 3 :]
    first, ghost, strip = scratch
    link = Link("gz", counts["gz"])
    lane = lane_ids()
    below, above = plane_in(link, got)
    settle(r2.at[0], r2s, top, tops, below, above, 0, link.after, first, ghost, strip, planes, rows)

    def step(t, later):
        row = pl.multiple_of(SUB * t + PAD, SUB)
        at, to = pl.ds(row, SUB), pl.ds(pl.multiple_of(SUB * t, SUB), SUB)
        spread = Around(chooser(r2, first, ghost, planes), strip, planes, row, lane)
        for k in range(planes):
            down = spread.steps(k)
            for a in range(3):
                later.put(grad, (a, k, to, ALL), x[a, k, at, :] + down[a])
            later.put(weight_grad, (k, to, ALL), wg[k, at, :])
            later.put(data_grad, (k, to, ALL), INVERSE * (dg[k, at, :] + spread.now[k]))

    in_groups(rows // SUB, LAST, step)


def call(body, counts, operands, outs, scratch=(), space=pltpu.VMEM, grant=16, aliases={}):
    held = pl.BlockSpec(memory_space=pltpu.VMEM)
    return pl.pallas_call(
        functools.partial(body, counts),
        out_shape=outs,
        in_specs=[pl.BlockSpec(memory_space=space)] * len(operands),
        out_specs=[held] * len(outs),
        scratch_shapes=list(scratch),
        compiler_params=pltpu.CompilerParams(vmem_limit_bytes=grant * 1024 * 1024),
        name=body.__name__,
        input_output_aliases=aliases,
        cost_estimate=pl.CostEstimate(flops=10**7, bytes_accessed=8 * 10**6, transcendentals=0),
    )(*operands)


def vmem(*shape):
    return pltpu.VMEM(shape, jnp.float32)


def shards(counts, data, weight, dual_start, dual_mid, cotangent):
    planes, rows, cols = data.shape
    held = rows + 2 * PAD
    tiles, flat, folded = sizes(rows)
    nx, ny, nz = (phases(counts[a]) for a in ("gx", "gy", "gz"))
    raw = (dual_mid, dual_start, cotangent, weight, data)
    block, strip, line = vmem(planes, held, cols), vmem(held, LANES), vmem(held, cols)

    far = [pltpu.with_memory_space_constraint(x, pltpu.HBM) for x in raw]
    sent = call(
        rows_out,
        counts,
        far,
        [vmem(planes * offsets()[1], cols)] * nx,
        [vmem(*x.shape[:-2], SUB, cols) for x in raw for _ in range(2)] + [pltpu.SemaphoreType.DMA((2 * len(raw),))],
        pltpu.HBM,
    )
    got = swap(sent, "gx", counts)
    mine = [vmem(FIELDS, planes, held, cols), vmem(FIELDS, held, LANES)] + [vmem(flat, LANES)] * ny
    part = call(inside, counts, far, mine, [pltpu.SemaphoreType.DMA((len(raw),))], pltpu.HBM)
    em, es, *sent = call(outside, counts, (*part, *got), mine, aliases={i: i for i in range(len(mine))})
    got = swap(sent, "gy", counts)
    one = flat + folded
    full, v, vs, *sent = call(
        strips_and_values,
        counts,
        (em, es, *got),
        [vmem(FIELDS, held, LANES), vmem(2, planes, held, cols), vmem(2, held, LANES)] + [vmem(2 * one, LANES)] * nz,
    )
    got_v = swap(sent, "gz", counts)
    state = [block, strip, block, strip, block, line, strip]
    work = [line, line, strip]
    *first, = call(
        first_step,
        counts,
        (em, full, v, vs, *got_v),
        state + [vmem(one, LANES)] * nz,
        work,
    )
    got_r = swap(first[7:], "gz", counts)
    *second, = call(
        second_step,
        counts,
        (em, full, v, vs, *got_v, *first[:7], *got_r),
        [vmem(3, planes, held, cols), block, strip, line, strip, block, block] + [vmem(one, LANES)] * nz,
        work + work,
    )
    got = swap(second[7:], "gz", counts)
    out = jax.ShapeDtypeStruct
    return tuple(call(
        finish,
        counts,
        (*second[:7], *got),
        [out(dual_mid.shape, jnp.float32), out(data.shape, jnp.float32), out(data.shape, jnp.float32)],
        work,
    ))


def solution(mesh):
    field, dual = P("gz", "gx", "gy"), P(None, "gz", "gx", "gy")
    return jax.shard_map(
        functools.partial(shards, dict(mesh.shape)),
        mesh=mesh,
        in_specs=(field, field, dual, dual, dual),
        out_specs=(dual, field, field),
        check_vma=False,
    )
```
